256 devices in a mesh: seq: 16 (over z, core), head: 16 (over x, y).
Axes of the slice: x: 4, y: 4, z: 8, core: 2. Of those that a mesh axis runs over, the one named last changes fastest.
Arguments:
- queries: bfloat16 [12288, 2048], P('seq', 'head'), may hold values from -8 to 8
- enc_keys: bfloat16 [32768, 2048], P('seq', 'head'), may hold values from -8 to 8
- enc_values: bfloat16 [32768, 2048], P('seq', 'head'), may hold values from -6 to 6
- out_proj: bfloat16 [2048, 2048], P('head'), may hold values from -0.125 to 0.125
- out_grad: bfloat16 [12288, 2048], P(('seq', 'head')), may hold values from -24 to 24
- block_doc: int32 [256], replicated, may hold values from 0 to 127, as said below
- query_doc: int32 [12288], replicated, may hold values from 0 to 127, as said below
Outputs:
- mixed: bfloat16 [12288, 2048], P(('seq', 'head'))
- grad_q: bfloat16 [12288, 2048], P('seq', 'head')
- grad_k: bfloat16 [32768, 2048], P('seq', 'head')
- grad_v: bfloat16 [32768, 2048], P('seq', 'head')
- grad_wo: float32 [2048, 2048], P('head', 'seq')
The draws below stay inside these ranges and needn't reach their ends.
Inputs may be any that keep to these rules, and one draw needn't show every extreme that they name: `block_doc`: never falls; each document's blocks are consecutive, lie on one sequence shard and number 1 to 3; each shard holds the blocks of exactly 8 documents. `query_doc`: every row belongs to a document; each document has 1 to 144 rows, all consecutive and on one sequence shard of 768 rows; each shard holds the rows of exactly 8 documents, and no two documents whose blocks lie on one shard have their rows on one shard.
All inputs are finite; a program needn't handle non-finite values.
Results may differ from the reference program's by a relative error of at most 0.023.
Values may be sent and summed in bfloat16 or wider, within the bound.
No kernel may reach another device: no remote copies, remote signals or barrier semaphores. Data moves between devices by JAX's collectives and lax.ppermute only.
A program may use at most 64 MiB of HBM per device.

```python
import jax
import jax.numpy as jnp
from jax import lax

D = 2048
HEADS = 32
HD = 64
INNER = 2048
BLOCK = 128
BLK = 16
DPS = 8
CAP = 3
Q_DEV = 768
QMOST = 144
NDOC = 128
ENC_TOK = 32768
Q_TOK = 12288
N_SEQ = 16


def layout(key):
    sub_keys = jax.random.split(jax.random.fold_in(key, 4099), 8)
    shards = N_SEQ
    shard_ids = jnp.arange(shards, dtype=jnp.int32)
    slot_ids = jnp.arange(DPS, dtype=jnp.int32)
    unit_rows = jnp.eye(DPS, dtype=jnp.int32)
    relabel = jax.random.permutation(sub_keys[0], shards).astype(jnp.int32)
    source_rank = jax.random.permutation(sub_keys[1], shards).astype(jnp.int32)
    offsets = jax.random.permutation(sub_keys[2], shards)[:DPS].astype(jnp.int32)
    position = (source_rank[:, None] + offsets[None, :]) % shards
    heavy_pair = position == 0
    shifted = jax.random.randint(sub_keys[3], (shards,), 0, DPS)
    block_shift = jnp.where(jnp.any(heavy_pair, axis=1), (DPS - jnp.argmax(heavy_pair, axis=1)) % DPS, shifted).astype(jnp.int32)
    first_move = jax.random.randint(sub_keys[4], (shards, 1), -1, 1)
    second_move = jax.random.randint(sub_keys[5], (shards, 1), -1, 1)
    block_pattern = jnp.array([3, 3, 2, 2, 2, 2, 1, 1], jnp.int32)[None, :] + first_move * (unit_rows[1] - unit_rows[5])[None, :] + second_move * (unit_rows[2] - unit_rows[6])[None, :]
    block_pick = (slot_ids[None, :] + block_shift[:, None]) % DPS
    block_lengths = jnp.take_along_axis(block_pattern, block_pick, axis=1)
    block_ends = jnp.cumsum(block_lengths, axis=1)
    local_block = jnp.arange(BLK, dtype=jnp.int32)
    block_slot = jnp.sum((local_block[None, :, None] >= block_ends[:, None, :]).astype(jnp.int32), axis=2)
    block_doc = (shard_ids[:, None] * DPS + block_slot).reshape(-1).astype(jnp.int32)
    inverse_relabel = jnp.zeros((shards,), jnp.int32).at[relabel].set(shard_ids)
    inverse_source = jnp.zeros((shards,), jnp.int32).at[source_rank].set(shard_ids)
    arriving = (inverse_relabel[:, None] - offsets[None, :]) % shards
    doc_here = inverse_source[arriving] * DPS + slot_ids[None, :]
    heavy_source = arriving == 0
    query_shifted = jax.random.randint(sub_keys[6], (shards,), 0, DPS)
    query_shift = jnp.where(jnp.any(heavy_source, axis=1), (DPS - jnp.argmax(heavy_source, axis=1)) % DPS, query_shifted).astype(jnp.int32)
    row_unit = Q_DEV // 32
    row_moves = jax.random.randint(sub_keys[7], (shards, 3), 1 - row_unit, row_unit)
    query_pattern = jnp.array([6, 5, 4, 4, 4, 3, 3, 3], jnp.int32)[None, :] * row_unit + row_moves[:, 0:1] * (unit_rows[1] - unit_rows[5])[None, :] + row_moves[:, 1:2] * (unit_rows[2] - unit_rows[6])[None, :] + row_moves[:, 2:3] * (unit_rows[3] - unit_rows[7])[None, :]
    query_pick = (slot_ids[None, :] + query_shift[:, None]) % DPS
    query_lengths = jnp.take_along_axis(query_pattern, query_pick, axis=1)
    query_ends = jnp.cumsum(query_lengths, axis=1)
    local_row = jnp.arange(Q_DEV, dtype=jnp.int32)
    row_slot = jnp.sum((local_row[None, :, None] >= query_ends[:, None, :]).astype(jnp.int32), axis=2)
    query_doc = jnp.take_along_axis(doc_here, row_slot, axis=1).reshape(-1).astype(jnp.int32)
    return (block_doc, query_doc)


def draw_block_doc(key, part):
    return layout(key)[0]


def draw_query_doc(key, part):
    return layout(key)[1]


def draw_queries(key, part):
    float_key = jax.random.fold_in(key, 31)
    drawn = jnp.clip(1.5 * jax.random.normal(float_key, (Q_TOK, INNER)), -8.0, 8.0)
    return drawn.astype(jnp.bfloat16)


def draw_enc_keys(key, part):
    float_key = jax.random.fold_in(key, 61)
    drawn = jnp.clip(jax.random.normal(float_key, (ENC_TOK, INNER)), -8.0, 8.0)
    return drawn.astype(jnp.bfloat16)


def strengthened(result, rng, source, target, parts, factor):
    def block_of(dim):
        return (jnp.arange(result.shape[dim]) // (result.shape[dim] // parts)).reshape((-1,) + (1,) * (result.ndim - 1 - dim))

    one_side = jax.random.permutation(rng, parts)[block_of(target)]
    far = (block_of(target) + parts // 2) % parts
    return jnp.where((block_of(source) == one_side) | (block_of(source) == far), factor * result, result)


def block_scale(key, dims, cuts, least, top_value):
    def one(dim, shards_of):
        steps = jax.random.uniform(jax.random.fold_in(jax.random.fold_in(key, 6), dim), (shards_of,), jnp.float32, least / len(cuts), top_value / len(cuts))
        return jnp.repeat(jnp.exp(steps), dims[dim] // shards_of).reshape((-1,) + (1,) * (len(dims) - dim - 1))

    level = one(*cuts[0])
    for cut in cuts[1:]:
        level = level * one(*cut)
    return level


def normal_values(rng, extent, spread, bound, cuts=(), kind=jnp.bfloat16):
    entries = spread * jax.random.normal(rng, extent, jnp.float32)
    if cuts:
        entries = entries * block_scale(rng, extent, cuts, -0.22, 0.18)
    return jnp.clip(entries, -bound, bound).astype(kind)


def noise_with(rng, extent, spread, reach, pieces, heavy, kind=jnp.bfloat16):
    result = spread * jax.random.normal(rng, extent, jnp.float32)
    if pieces:
        result = result * block_scale(rng, extent, pieces, -0.22, 0.18)
    return jnp.clip(strengthened(result, jax.random.fold_in(rng, 3), *heavy), -reach, reach).astype(kind)


def setup_inputs(seed: int = 0) -> dict:
    streams_of = jax.random.split(jax.random.key(seed), 8)
    return {
        "queries": draw_queries(jax.random.fold_in(streams_of[7], 71), 0),
        "enc_keys": draw_enc_keys(jax.random.fold_in(streams_of[7], 71), 0),
        "enc_values": normal_values(streams_of[2], (ENC_TOK, INNER), 1.0, 6.0, ((0, 16), (1, 16))),
        "out_proj": normal_values(streams_of[3], (INNER, D), INNER ** -0.5, 0.125, ((0, 16),)),
        "out_grad": noise_with(streams_of[4], (Q_TOK, D), 1.0, 24.0, ((0, 256),), (0, 1, 256, 6.0)),
        "block_doc": draw_block_doc(jax.random.fold_in(streams_of[7], 71), 0),
        "query_doc": draw_query_doc(jax.random.fold_in(streams_of[7], 71), 0),
    }


score_scale = 0.125
masked_score = -1.0e30


def reference(queries, enc_keys, enc_values, out_proj, out_grad, block_doc, query_doc):
    query_total = queries.shape[0]
    block_total = block_doc.shape[0]
    enc_total = enc_keys.shape[0]
    attn_grad = jnp.dot(out_grad, out_proj.T, preferred_element_type=jnp.float32).astype(jnp.bfloat16)
    token_span = jnp.arange(BLOCK, dtype=jnp.int32)

    def one_doc(doc_id):
        picked_rows = jnp.nonzero(query_doc == doc_id, size=QMOST, fill_value=query_total)[0].astype(jnp.int32)
        row_valid = picked_rows < query_total
        row_index = jnp.minimum(picked_rows, query_total - 1).astype(jnp.int32)
        picked_blocks = jnp.nonzero(block_doc == doc_id, size=CAP, fill_value=block_total)[0].astype(jnp.int32)
        block_valid = picked_blocks < block_total
        token_index = (jnp.minimum(picked_blocks, block_total - 1)[:, None] * BLOCK + token_span[None, :]).reshape(-1).astype(jnp.int32)
        token_valid = jnp.repeat(block_valid, BLOCK)
        query_rows = queries[row_index].astype(jnp.float32).reshape(QMOST, HEADS, HD)
        key_rows = enc_keys[token_index].astype(jnp.float32).reshape(CAP * BLOCK, HEADS, HD)
        value_rows = enc_values[token_index].astype(jnp.float32).reshape(CAP * BLOCK, HEADS, HD)
        grad_rows = attn_grad[row_index].astype(jnp.float32).reshape(QMOST, HEADS, HD)
        scores = jnp.einsum("qhd,khd->hqk", query_rows, key_rows) * score_scale
        admitted = (row_valid[:, None] & token_valid[None, :])[None, :, :]
        masked = jnp.where(admitted, scores, masked_score)
        row_max = jnp.max(masked, axis=2)
        row_sum = jnp.sum(jnp.where(admitted, jnp.exp(masked - row_max[:, :, None]), 0.0), axis=2)
        row_sum = row_sum + (1.0 - row_valid.astype(jnp.float32))[None, :]
        logsum = row_max + jnp.log(row_sum)
        probs = jnp.where(admitted, jnp.exp(scores - logsum[:, :, None]), 0.0)
        weights = lax.optimization_barrier(probs.astype(jnp.bfloat16)).astype(jnp.float32)
        attended = jnp.einsum("hqk,khd->qhd", weights, value_rows).astype(jnp.bfloat16)
        attended_wide = lax.optimization_barrier(attended).astype(jnp.float32)
        row_delta = jnp.sum(grad_rows * attended_wide, axis=2)
        dprobs = jnp.einsum("qhd,khd->hqk", grad_rows, value_rows)
        dscores = (probs * (dprobs - row_delta.T[:, :, None])).astype(jnp.bfloat16)
        dscores = lax.optimization_barrier(dscores).astype(jnp.float32)
        query_grads = (jnp.einsum("hqk,khd->qhd", dscores, key_rows) * score_scale).astype(jnp.bfloat16)
        key_grads = (jnp.einsum("hqk,qhd->khd", dscores, query_rows) * score_scale).astype(jnp.bfloat16)
        value_grads = jnp.einsum("hqk,qhd->khd", weights, grad_rows).astype(jnp.bfloat16)
        row_target = jnp.where(row_valid, picked_rows, query_total).astype(jnp.int32)
        token_target = jnp.where(token_valid, token_index, enc_total).astype(jnp.int32)
        return (row_target, token_target, attended.reshape(QMOST, INNER), query_grads.reshape(QMOST, INNER),
                key_grads.reshape(CAP * BLOCK, INNER), value_grads.reshape(CAP * BLOCK, INNER))

    row_target, token_target, attended, query_grads, key_grads, value_grads = lax.map(one_doc, jnp.arange(NDOC, dtype=jnp.int32))
    flat_rows = row_target.reshape(-1)
    flat_tokens = token_target.reshape(-1)
    attended_all = jnp.zeros((query_total, INNER), jnp.bfloat16).at[flat_rows].set(attended.reshape(-1, INNER), mode="drop")
    grad_q = jnp.zeros((query_total, INNER), jnp.bfloat16).at[flat_rows].set(query_grads.reshape(-1, INNER), mode="drop")
    grad_k = jnp.zeros((enc_total, INNER), jnp.bfloat16).at[flat_tokens].set(key_grads.reshape(-1, INNER), mode="drop")
    grad_v = jnp.zeros((enc_total, INNER), jnp.bfloat16).at[flat_tokens].set(value_grads.reshape(-1, INNER), mode="drop")
    mixed = jnp.dot(attended_all, out_proj, preferred_element_type=jnp.float32).astype(jnp.bfloat16)
    grad_wo = jnp.dot(attended_all.T, out_grad, preferred_element_type=jnp.float32)
    return mixed, grad_q, grad_k, grad_v, grad_wo
```

```python
import jax
import jax.numpy as jnp
from jax import lax
from jax.experimental import pallas as pl
from jax.experimental.pallas import tpu as pltpu
from jax.sharding import PartitionSpec as P

BLOCK = 128
DPS = 8
SLOT = 144
N_SEQ = 16
SIDE = 4
LANE_SPLIT = 64
SCALE = 0.125

VMEM = pltpu.MemorySpace.VMEM
SMEM = pltpu.MemorySpace.SMEM


def vmem_specs(count):
    return [pl.BlockSpec(memory_space=VMEM)] * count


def smem_specs(count):
    return [pl.BlockSpec(memory_space=SMEM)] * count


def dot(a, b, dims):
    return lax.dot_general(a, b, (dims, ((), ())), preferred_element_type=jnp.float32)


def select(equal):
    return jnp.where(equal, 1.0, 0.0).astype(jnp.bfloat16)


def pack_rows(slot_row, rows, out_ref):
    for slot in range(N_SEQ):
        place = lax.broadcasted_iota(jnp.int32, (SLOT, slot_row.shape[1]), 0) + slot * SLOT
        out_ref[slot] = dot(select(place == slot_row), rows, ((1,), (0,))).astype(jnp.bfloat16)


def unpack_rows(slot_col, packed):
    place = lax.broadcasted_iota(jnp.int32, (slot_col.shape[0], packed.shape[0]), 1)
    return dot(select(place == slot_col), packed, ((1,), (0,))).astype(jnp.bfloat16)


def pack_kernel(slot_ref, rows_ref, out_ref):
    pack_rows(slot_ref[...], rows_ref[...], out_ref)


def pack_queries(slot_row, queries):
    return pl.pallas_call(
        pack_kernel,
        out_shape=jax.ShapeDtypeStruct((N_SEQ, SLOT, queries.shape[1]), jnp.bfloat16),
        in_specs=vmem_specs(2),
        out_specs=pl.BlockSpec(memory_space=VMEM),
        name="pack_queries",
    )(slot_row, queries)


def unpack_kernel(slot_ref, packed_ref, out_ref):
    packed = packed_ref[...].reshape(N_SEQ * SLOT, -1)
    step = out_ref.shape[0] // SIDE
    for part in range(SIDE):
        span = slice(part * step, (part + 1) * step)
        out_ref[span, :] = unpack_rows(slot_ref[span, :], packed)


def unpack_grads(slot_col, packed):
    return pl.pallas_call(
        unpack_kernel,
        out_shape=jax.ShapeDtypeStruct((slot_col.shape[0], packed.shape[2]), jnp.bfloat16),
        in_specs=vmem_specs(2),
        out_specs=pl.BlockSpec(memory_space=VMEM),
        name="unpack_grads",
    )(slot_col, packed)


def swap_order(rows):
    unit = rows.shape[0] // (SIDE * SIDE)
    return jnp.concatenate(
        [
            rows[(a * SIDE + b) * unit : (a * SIDE + b + 1) * unit]
            for b in range(SIDE)
            for a in range(SIDE)
        ],
        axis=0,
    )


def grad_kernel(slot_ref, proj_ref, *refs):
    first, second, out_ref = refs[:SIDE], refs[SIDE : 2 * SIDE], refs[2 * SIDE]
    half = proj_ref.shape[1] // 2
    low = proj_ref[:, :half]
    high = proj_ref[:, half:]
    one = jnp.concatenate([dot(r[...], low, ((1,), (1,))) for r in first], axis=0)
    two = jnp.concatenate([dot(r[...], high, ((1,), (1,))) for r in second], axis=0)
    grads = (one + swap_order(two)).astype(jnp.bfloat16)
    pack_rows(slot_ref[...], grads, out_ref)


def attention_grads(slot_row, out_proj, first, second):
    return pl.pallas_call(
        grad_kernel,
        out_shape=jax.ShapeDtypeStruct((N_SEQ, SLOT, out_proj.shape[0]), jnp.bfloat16),
        in_specs=vmem_specs(2 + 2 * SIDE),
        out_specs=pl.BlockSpec(memory_space=VMEM),
        name="attention_grads",
    )(slot_row, out_proj, *first, *second)


def two_heads(rows):
    low = lax.broadcasted_iota(jnp.int32, rows.shape, 1) < LANE_SPLIT
    zero = jnp.zeros_like(rows)
    return jnp.concatenate([jnp.where(low, rows, zero), jnp.where(low, zero, rows)], axis=0)


def one_row(stacked):
    half = stacked.shape[0] // 2
    low = lax.broadcasted_iota(jnp.int32, (half, stacked.shape[1]), 1) < LANE_SPLIT
    return jnp.where(low, stacked[:half], stacked[half:])


def for_documents(source_ref, start_ref, count_ref, body):
    def step(doc, carry):
        source = source_ref[doc]
        first = pl.multiple_of(start_ref[doc] * BLOCK, BLOCK)
        for blocks in range(1, 4):

            @pl.when(count_ref[doc] == blocks)
            def _():
                body(doc, source, pl.ds(first, blocks * BLOCK), blocks * BLOCK)

        return carry

    lax.fori_loop(0, DPS, step, 0)


def forward_kernel(source_ref, start_ref, count_ref, q_ref, k_ref, v_ref, att_ref, w_ref):
    att_ref[...] = jnp.zeros(att_ref.shape, att_ref.dtype)

    def body(doc, source, tokens, width):
        queries = two_heads(q_ref[source])
        scores = dot(queries, k_ref[tokens, :], ((1,), (1,))) * SCALE
        top = jnp.max(scores, axis=1, keepdims=True)
        terms = jnp.exp(scores - top)
        weights = (terms / jnp.sum(terms, axis=1, keepdims=True)).astype(jnp.bfloat16)
        w_ref[doc, :, :width] = weights
        mixed = dot(weights, v_ref[tokens, :], ((1,), (0,)))
        att_ref[source] = one_row(mixed).astype(jnp.bfloat16)

    for_documents(source_ref, start_ref, count_ref, body)


def forward(source, start, count, got_q, keys, values):
    return pl.pallas_call(
        forward_kernel,
        out_shape=(
            jax.ShapeDtypeStruct(got_q.shape, jnp.bfloat16),
            jax.ShapeDtypeStruct((DPS, 2 * SLOT, 3 * BLOCK), jnp.bfloat16),
        ),
        in_specs=smem_specs(3) + vmem_specs(3),
        out_specs=tuple(vmem_specs(2)),
        name="forward",
    )(source, start, count, got_q, keys, values)


def backward_kernel(
    source_ref, start_ref, count_ref, q_ref, g_ref, att_ref, w_ref, k_ref, v_ref, dq_ref, dk_ref, dv_ref
):
    dq_ref[...] = jnp.zeros(dq_ref.shape, dq_ref.dtype)

    def body(doc, source, tokens, width):
        queries = two_heads(q_ref[source])
        grads = two_heads(g_ref[source])
        attended = att_ref[source].astype(jnp.float32)
        both = jnp.concatenate([attended, attended], axis=0)
        delta = jnp.sum(grads.astype(jnp.float32) * both, axis=1, keepdims=True)
        weights = w_ref[doc, :, :width]
        dprobs = dot(grads, v_ref[tokens, :], ((1,), (1,)))
        dscores = (weights.astype(jnp.float32) * (dprobs - delta)).astype(jnp.bfloat16)
        dq = dot(dscores, k_ref[tokens, :], ((1,), (0,)))
        dq_ref[source] = (one_row(dq) * SCALE).astype(jnp.bfloat16)
        dk_ref[tokens, :] = (dot(dscores, queries, ((0,), (0,))) * SCALE).astype(jnp.bfloat16)
        dv_ref[tokens, :] = dot(weights, grads, ((0,), (0,))).astype(jnp.bfloat16)

    for_documents(source_ref, start_ref, count_ref, body)


def backward(source, start, count, got_q, got_g, attended, weights, keys, values):
    return pl.pallas_call(
        backward_kernel,
        out_shape=(
            jax.ShapeDtypeStruct(got_q.shape, jnp.bfloat16),
            jax.ShapeDtypeStruct(keys.shape, jnp.bfloat16),
            jax.ShapeDtypeStruct(values.shape, jnp.bfloat16),
        ),
        in_specs=smem_specs(3) + vmem_specs(6),
        out_specs=tuple(vmem_specs(3)),
        name="backward",
    )(source, start, count, got_q, got_g, attended, weights, keys, values)


def mixed_kernel(slot_ref, packed_ref, proj_ref, *refs):
    first, second = refs[:SIDE], refs[SIDE : 2 * SIDE]
    m_first, m_second = refs[2 * SIDE : 3 * SIDE], refs[3 * SIDE : 4 * SIDE]
    even_ref, odd_ref = refs[4 * SIDE :]
    packed = packed_ref[...].reshape(N_SEQ * SLOT, -1)
    step = slot_ref.shape[0] // SIDE
    half = proj_ref.shape[1] // 2
    rows = [unpack_rows(slot_ref[p * step : (p + 1) * step, :], packed) for p in range(SIDE)]
    other = swap_order(jnp.concatenate(rows, axis=0))
    rows_two = [other[p * step : (p + 1) * step] for p in range(SIDE)]
    sums = []
    for part, ins, outs, cols in (
        (rows, first, m_first, slice(0, half)),
        (rows_two, second, m_second, slice(half, 2 * half)),
    ):
        total = None
        for p in range(SIDE):
            outs[p][...] = dot(part[p], proj_ref[:, cols], ((1,), (0,))).astype(jnp.bfloat16)
            term = dot(part[p], ins[p][...], ((0,), (0,)))
            total = term if total is None else total + term
        sums.append(total)
    per_half = half // BLOCK
    for h in range(2):
        for c in range(per_half):
            chunk = h * per_half + c
            target = even_ref if chunk % 2 == 0 else odd_ref
            target[chunk // 2] = sums[h][:, c * BLOCK : (c + 1) * BLOCK]


def mixed_parts(slot_col, packed, out_proj, first, second):
    inner, width = out_proj.shape
    part = jax.ShapeDtypeStruct(first[0].shape, jnp.bfloat16)
    sums = jax.ShapeDtypeStruct((width // BLOCK // 2, inner, BLOCK), jnp.float32)
    outs = pl.pallas_call(
        mixed_kernel,
        out_shape=(part,) * (2 * SIDE) + (sums,) * 2,
        in_specs=vmem_specs(3 + 2 * SIDE),
        out_specs=tuple(vmem_specs(2 * SIDE + 2)),
        name="mixed_parts",
    )(slot_col, packed, out_proj, *first, *second)
    return outs[:SIDE], outs[SIDE : 2 * SIDE], outs[2 * SIDE], outs[2 * SIDE + 1]


def along_x(value, k):
    perm = [(x * SIDE + y, (x + k) % SIDE * SIDE + y) for x in range(SIDE) for y in range(SIDE)]
    return lax.ppermute(value, "head", perm)


def along_y(value, k):
    perm = [(x * SIDE + y, x * SIDE + (y + k) % SIDE) for x in range(SIDE) for y in range(SIDE)]
    return lax.ppermute(value, "head", perm)


def gather(value, one, two):
    rows = jnp.concatenate([value] + [one(value, k) for k in range(1, SIDE)], axis=0)
    return [rows] + [two(rows, k) for k in range(1, SIDE)]


def total(parts):
    out = parts[0].astype(jnp.float32)
    for part in parts[1:]:
        out = out + part.astype(jnp.float32)
    return out.astype(jnp.bfloat16)


def scatter_sum(parts, one, two):
    rows = total([parts[0]] + [one(parts[k], SIDE - k) for k in range(1, SIDE)])
    unit = rows.shape[0] // SIDE
    return total(
        [rows[:unit]]
        + [two(rows[k * unit : (k + 1) * unit], SIDE - k) for k in range(1, SIDE)]
    )


def to_all(value):
    return lax.all_to_all(value, "seq", split_axis=0, concat_axis=0, tiled=True)


def shards(queries, enc_keys, enc_values, out_proj, out_grad, block_doc, query_doc):
    shard = lax.axis_index("seq")
    head = lax.axis_index("head")
    row_count = queries.shape[0]
    half = out_grad.shape[1] // 2
    rows = jnp.arange(row_count, dtype=jnp.int32)

    docs_here = lax.dynamic_slice_in_dim(query_doc, shard * row_count, row_count)
    same = docs_here[:, None] == docs_here[None, :]
    slot_row = docs_here // DPS * SLOT + rows - jnp.min(jnp.where(same, rows[:, None], row_count), axis=0)
    got_q = to_all(pack_queries(slot_row[None, :], queries))

    first = gather(out_grad[:, :half], along_x, along_y)
    second = gather(out_grad[:, half:], along_y, along_x)

    unit = out_grad.shape[0]
    block = rows // unit
    behind_y, behind_x = block // SIDE, block % SIDE
    source_block = (head // SIDE - behind_x) % SIDE * SIDE + (head % SIDE - behind_y) % SIDE
    source_row = source_block * unit + rows % unit
    slot_rel = jnp.sum(jnp.where(source_row[None, :] == rows[:, None], slot_row[:, None], 0), axis=0)
    slot_rel_col = jnp.sum(jnp.where(source_row[:, None] == rows[None, :], slot_row[None, :], 0), axis=1)

    my_docs = shard * DPS + jnp.arange(DPS, dtype=jnp.int32)
    all_rows = jnp.arange(query_doc.shape[0], dtype=jnp.int32)
    source = jnp.max(jnp.where(query_doc[None, :] == my_docs[:, None], all_rows[None, :], 0), axis=1) // row_count
    local_blocks = enc_keys.shape[0] // BLOCK
    blocks_here = lax.dynamic_slice_in_dim(block_doc, shard * local_blocks, local_blocks)
    start = jnp.sum((blocks_here[None, :] < my_docs[:, None]).astype(jnp.int32), axis=1)
    count = jnp.sum((blocks_here[None, :] == my_docs[:, None]).astype(jnp.int32), axis=1)

    attended, weights = forward(source, start, count, got_q, enc_keys, enc_values)
    home = to_all(attended)
    got_g = to_all(attention_grads(slot_rel[None, :], out_proj, first, second))

    m_first, m_second, even, odd = mixed_parts(slot_rel_col[:, None], home, out_proj, first, second)
    mixed = jnp.concatenate(
        [scatter_sum(m_first, along_y, along_x), scatter_sum(m_second, along_x, along_y)], axis=1
    )

    core = shard % 2
    swap = [(s, s ^ 1) for s in range(N_SEQ)]
    other = lax.ppermute(jnp.where(core == 0, odd, even).astype(jnp.bfloat16), "seq", swap)
    pair = (jnp.where(core == 0, even, odd) + other.astype(jnp.float32)).astype(jnp.bfloat16)
    groups = [[z * 2 + c for z in range(N_SEQ // 2)] for c in range(2)]
    terms = lax.all_to_all(pair, "seq", split_axis=0, concat_axis=0, axis_index_groups=groups, tiled=True)
    grad_wo = jnp.sum(terms.astype(jnp.float32), axis=0)

    grads_q, grad_k, grad_v = backward(
        source, start, count, got_q, got_g, attended, weights, enc_keys, enc_values
    )
    grad_q = unpack_grads(slot_row[:, None], to_all(grads_q))
    return (mixed, grad_q, grad_k, grad_v, grad_wo)


def solution(mesh):
    placed = (
        P("seq", "head"),
        P("seq", "head"),
        P("seq", "head"),
        P("head", None),
        P(("seq", "head"), None),
        P(),
        P(),
    )
    return jax.shard_map(
        shards,
        mesh=mesh,
        in_specs=placed,
        out_specs=(
            P(("seq", "head"), None),
            P("seq", "head"),
            P("seq", "head"),
            P("seq", "head"),
            P("head", "seq"),
        ),
        check_vma=False,
    )
```

```python
import jax
import jax.numpy as jnp
from jax import lax
from jax.experimental import pallas as pl
from jax.experimental.pallas import tpu as pltpu
from jax.sharding import PartitionSpec as P


BLOCK = 128
DPS = 8
SLOT = 144
TILE = 16
WINDOW = SLOT + TILE
CAP = 3
MASKED = -1e30
N_SEQ = 16
SIDE = 4
LANE_SPLIT = 64
SCALE = 0.125

VMEM = pltpu.MemorySpace.VMEM
SMEM = pltpu.MemorySpace.SMEM


def vmem_specs(count):
    return [pl.BlockSpec(memory_space=VMEM)] * count


def smem_specs(count):
    return [pl.BlockSpec(memory_space=SMEM)] * count


def dot(a, b, dims):
    return lax.dot_general(a, b, (dims, ((), ())), preferred_element_type=jnp.float32)


def select(equal):
    return jnp.where(equal, 1.0, 0.0).astype(jnp.bfloat16)


def window(start_ref, slot, row_count):
    start = start_ref[slot]
    base = pl.multiple_of(jnp.minimum(start // TILE * TILE, row_count - WINDOW), TILE)
    return pl.ds(base, WINDOW), start - base


def pack_rows(start_ref, count_ref, rows_ref, out_ref):
    lane = lax.broadcasted_iota(jnp.int32, (SLOT, WINDOW), 1)
    row = lax.broadcasted_iota(jnp.int32, (SLOT, WINDOW), 0)
    ahead = lane - row

    def step(slot, carry):
        span, skip = window(start_ref, slot, rows_ref.shape[0])
        chosen = select((ahead == skip) & (row < count_ref[slot]))
        out_ref[slot] = dot(chosen, rows_ref[span, :], ((1,), (0,))).astype(jnp.bfloat16)
        return carry

    lax.fori_loop(0, N_SEQ, step, 0, unroll=4)


def unpack_rows(start_ref, count_ref, packed_ref, sum_ref):
    lane = lax.broadcasted_iota(jnp.int32, (WINDOW, SLOT), 1)
    row = lax.broadcasted_iota(jnp.int32, (WINDOW, SLOT), 0)
    ahead = row - lane
    sum_ref[...] = jnp.zeros(sum_ref.shape, sum_ref.dtype)

    def step(slot, carry):
        span, skip = window(start_ref, slot, sum_ref.shape[0])
        chosen = select((ahead == skip) & (lane < count_ref[slot]))
        sum_ref[span, :] += dot(chosen, packed_ref[slot], ((1,), (0,)))
        return carry

    lax.fori_loop(0, N_SEQ, step, 0, unroll=4)


def block_rows(head_ref, behind_x, behind_y, unit):
    x, y = head_ref[0] // SIDE, head_ref[0] % SIDE
    block = (x + SIDE - behind_x) % SIDE * SIDE + (y + SIDE - behind_y) % SIDE
    return pl.ds(pl.multiple_of(block * unit, TILE), unit)


def pack_queries(start, count, queries):
    return pl.pallas_call(
        pack_rows,
        out_shape=jax.ShapeDtypeStruct((N_SEQ, SLOT, queries.shape[1]), jnp.bfloat16),
        in_specs=smem_specs(2) + vmem_specs(1),
        out_specs=pl.BlockSpec(memory_space=VMEM),
        name="pack_queries",
    )(start, count, queries)


def unpack_kernel(start_ref, count_ref, packed_ref, out_ref, sum_ref):
    unpack_rows(start_ref, count_ref, packed_ref, sum_ref)
    out_ref[...] = sum_ref[...].astype(jnp.bfloat16)


def unpack_grads(start, count, packed, row_count):
    shape = (row_count, packed.shape[2])
    return pl.pallas_call(
        unpack_kernel,
        out_shape=jax.ShapeDtypeStruct(shape, jnp.bfloat16),
        in_specs=smem_specs(2) + vmem_specs(1),
        out_specs=pl.BlockSpec(memory_space=VMEM),
        scratch_shapes=[pltpu.VMEM(shape, jnp.float32)],
        name="unpack_grads",
    )(start, count, packed)


def grad_kernel(start_ref, count_ref, head_ref, proj_ref, *refs):
    first, second, out_ref, rows_ref = refs[:SIDE], refs[SIDE : 2 * SIDE], refs[2 * SIDE], refs[2 * SIDE + 1]
    half = proj_ref.shape[1] // 2
    unit = rows_ref.shape[0] // (SIDE * SIDE)
    low = proj_ref[:, :half]
    high = proj_ref[:, half:]
    one = [dot(r[...], low, ((1,), (1,))) for r in first]
    two = [dot(r[...], high, ((1,), (1,))) for r in second]
    for a in range(SIDE):
        for b in range(SIDE):
            grads = one[a][b * unit : (b + 1) * unit] + two[b][a * unit : (a + 1) * unit]
            rows_ref[block_rows(head_ref, b, a, unit), :] = grads.astype(jnp.bfloat16)
    pack_rows(start_ref, count_ref, rows_ref, out_ref)


def attention_grads(start, count, head, out_proj, first, second):
    inner = out_proj.shape[0]
    row_count = SIDE * first[0].shape[0]
    return pl.pallas_call(
        grad_kernel,
        out_shape=jax.ShapeDtypeStruct((N_SEQ, SLOT, inner), jnp.bfloat16),
        in_specs=smem_specs(3) + vmem_specs(1 + 2 * SIDE),
        out_specs=pl.BlockSpec(memory_space=VMEM),
        scratch_shapes=[pltpu.VMEM((row_count, inner), jnp.bfloat16)],
        name="attention_grads",
    )(start, count, head, out_proj, *first, *second)


def two_heads(rows):
    low = lax.broadcasted_iota(jnp.int32, rows.shape, 1) < LANE_SPLIT
    zero = jnp.zeros_like(rows)
    return jnp.concatenate([jnp.where(low, rows, zero), jnp.where(low, zero, rows)], axis=0)


def one_row(stacked):
    half = stacked.shape[0] // 2
    low = lax.broadcasted_iota(jnp.int32, (half, stacked.shape[1]), 1) < LANE_SPLIT
    return jnp.where(low, stacked[:half], stacked[half:])


def document(refs, doc, block_total):
    source_ref, start_ref, count_ref = refs
    start = start_ref[doc]
    base = jnp.minimum(start, block_total - CAP)
    return source_ref[doc], base, start - base, count_ref[doc]


def forward_kernel(source_ref, start_ref, count_ref, q_ref, k_ref, v_ref, att_ref, w_ref):
    att_ref[...] = jnp.zeros(att_ref.shape, att_ref.dtype)
    refs = (source_ref, start_ref, count_ref)
    lane = lax.broadcasted_iota(jnp.int32, (1, CAP * BLOCK), 1)
    for doc in range(DPS):
        source, base, skip, count = document(refs, doc, k_ref.shape[0] // BLOCK)
        tokens = pl.ds(pl.multiple_of(base * BLOCK, BLOCK), CAP * BLOCK)
        admitted = (lane >= skip * BLOCK) & (lane < (skip + count) * BLOCK)
        queries = two_heads(q_ref[source])
        scores = dot(queries, k_ref[tokens, :], ((1,), (1,))) * SCALE
        scores = jnp.where(admitted, scores, MASKED)
        top = jnp.max(scores, axis=1, keepdims=True)
        terms = jnp.exp(scores - top)
        scale = 1.0 / jnp.sum(terms, axis=1, keepdims=True)
        weights = (terms * scale).astype(jnp.bfloat16)
        w_ref[doc] = weights
        mixed = dot(weights, v_ref[tokens, :], ((1,), (0,)))
        att_ref[source] = one_row(mixed).astype(jnp.bfloat16)


def forward(source, start, count, got_q, keys, values):
    return pl.pallas_call(
        forward_kernel,
        out_shape=(
            jax.ShapeDtypeStruct(got_q.shape, jnp.bfloat16),
            jax.ShapeDtypeStruct((DPS, 2 * SLOT, 3 * BLOCK), jnp.bfloat16),
        ),
        in_specs=smem_specs(3) + vmem_specs(3),
        out_specs=tuple(vmem_specs(2)),
        name="forward",
    )(source, start, count, got_q, keys, values)


def backward_kernel(
    source_ref, start_ref, count_ref, q_ref, g_ref, att_ref, w_ref, k_ref, v_ref, dq_ref, dk_ref, dv_ref
):
    dq_ref[...] = jnp.zeros(dq_ref.shape, dq_ref.dtype)
    refs = (source_ref, start_ref, count_ref)
    for doc in range(DPS):
        source, base, skip, _ = document(refs, doc, k_ref.shape[0] // BLOCK)
        tokens = pl.ds(pl.multiple_of(base * BLOCK, BLOCK), CAP * BLOCK)
        queries = two_heads(q_ref[source])
        grads = two_heads(g_ref[source])
        attended = att_ref[source].astype(jnp.float32)
        both = jnp.concatenate([attended, attended], axis=0)
        delta = jnp.sum(grads.astype(jnp.float32) * both, axis=1, keepdims=True)
        weights = w_ref[doc]
        dprobs = dot(grads, v_ref[tokens, :], ((1,), (1,)))
        dscores = (weights.astype(jnp.float32) * (dprobs - delta)).astype(jnp.bfloat16)
        dq = dot(dscores, k_ref[tokens, :], ((1,), (0,)))
        dq_ref[source] = (one_row(dq) * SCALE).astype(jnp.bfloat16)
        dk = (dot(dscores, queries, ((0,), (0,))) * SCALE).astype(jnp.bfloat16)
        dv = dot(weights, grads, ((0,), (0,))).astype(jnp.bfloat16)
        for part in range(CAP):
            rows = pl.ds(pl.multiple_of((base + part) * BLOCK, BLOCK), BLOCK)
            span = slice(part * BLOCK, (part + 1) * BLOCK)
            if part == CAP - 1:
                dk_ref[rows, :] = dk[span]
                dv_ref[rows, :] = dv[span]
            else:
                keep = skip > part
                dk_ref[rows, :] = jnp.where(keep, dk_ref[rows, :], dk[span])
                dv_ref[rows, :] = jnp.where(keep, dv_ref[rows, :], dv[span])


def backward(source, start, count, got_q, got_g, attended, weights, keys, values):
    return pl.pallas_call(
        backward_kernel,
        out_shape=(
            jax.ShapeDtypeStruct(got_q.shape, jnp.bfloat16),
            jax.ShapeDtypeStruct(keys.shape, jnp.bfloat16),
            jax.ShapeDtypeStruct(values.shape, jnp.bfloat16),
        ),
        in_specs=smem_specs(3) + vmem_specs(6),
        out_specs=tuple(vmem_specs(3)),
        name="backward",
    )(source, start, count, got_q, got_g, attended, weights, keys, values)


def mixed_kernel(start_ref, count_ref, head_ref, packed_ref, proj_ref, *refs):
    first, second = refs[:SIDE], refs[SIDE : 2 * SIDE]
    m_first, m_second = refs[2 * SIDE : 3 * SIDE], refs[3 * SIDE : 4 * SIDE]
    even_ref, odd_ref, sum_ref = refs[4 * SIDE :]
    unpack_rows(start_ref, count_ref, packed_ref, sum_ref)
    unit = sum_ref.shape[0] // (SIDE * SIDE)
    half = proj_ref.shape[1] // 2
    blocks = [
        [sum_ref[block_rows(head_ref, b, a, unit), :].astype(jnp.bfloat16) for b in range(SIDE)]
        for a in range(SIDE)
    ]
    rows = [jnp.concatenate(blocks[a], axis=0) for a in range(SIDE)]
    rows_two = [jnp.concatenate([blocks[a][b] for a in range(SIDE)], axis=0) for b in range(SIDE)]
    sums = []
    for part, ins, outs, cols in (
        (rows, first, m_first, slice(0, half)),
        (rows_two, second, m_second, slice(half, 2 * half)),
    ):
        term = None
        for p in range(SIDE):
            outs[p][...] = dot(part[p], proj_ref[:, cols], ((1,), (0,))).astype(jnp.bfloat16)
            more = dot(part[p], ins[p][...], ((0,), (0,)))
            term = more if term is None else term + more
        sums.append(term)
    per_half = half // BLOCK
    for h in range(2):
        for c in range(per_half):
            chunk = h * per_half + c
            target = even_ref if chunk % 2 == 0 else odd_ref
            target[chunk // 2] = sums[h][:, c * BLOCK : (c + 1) * BLOCK]


def mixed_parts(start, count, head, packed, out_proj, first, second):
    inner, width = out_proj.shape
    row_count = SIDE * first[0].shape[0]
    part = jax.ShapeDtypeStruct(first[0].shape, jnp.bfloat16)
    sums = jax.ShapeDtypeStruct((width // BLOCK // 2, inner, BLOCK), jnp.float32)
    outs = pl.pallas_call(
        mixed_kernel,
        out_shape=(part,) * (2 * SIDE) + (sums,) * 2,
        in_specs=smem_specs(3) + vmem_specs(2 + 2 * SIDE),
        out_specs=tuple(vmem_specs(2 * SIDE + 2)),
        scratch_shapes=[pltpu.VMEM((row_count, inner), jnp.float32)],
        name="mixed_parts",
    )(start, count, head, packed, out_proj, *first, *second)
    return outs[:SIDE], outs[SIDE : 2 * SIDE], outs[2 * SIDE], outs[2 * SIDE + 1]


def along_x(value, k):
    perm = [(x * SIDE + y, (x + k) % SIDE * SIDE + y) for x in range(SIDE) for y in range(SIDE)]
    return lax.ppermute(value, "head", perm)


def along_y(value, k):
    perm = [(x * SIDE + y, x * SIDE + (y + k) % SIDE) for x in range(SIDE) for y in range(SIDE)]
    return lax.ppermute(value, "head", perm)


def along_z(value, k):
    perm = [(s, (s + 2 * k) % N_SEQ) for s in range(N_SEQ)]
    return lax.ppermute(value, "seq", perm)


def shift(value, move, k):
    return move(value, k)


def gather(value, one, two):
    rows = jnp.concatenate([value] + [shift(value, one, k) for k in range(1, SIDE)], axis=0)
    return [rows] + [shift(rows, two, k) for k in range(1, SIDE)]


def total(parts):
    out = parts[0].astype(jnp.float32)
    for part in parts[1:]:
        out = out + part.astype(jnp.float32)
    return out.astype(jnp.bfloat16)


def scatter_sum(parts, one, two):
    rows = total([parts[0]] + [shift(parts[k], one, SIDE - k) for k in range(1, SIDE)])
    unit = rows.shape[0] // SIDE
    return total(
        [rows[:unit]]
        + [shift(rows[k * unit : (k + 1) * unit], two, SIDE - k) for k in range(1, SIDE)]
    )


def to_all(value):
    return lax.all_to_all(value, "seq", split_axis=0, concat_axis=0, tiled=True)


def work(queries, enc_keys, enc_values, out_proj, out_grad, block_doc, query_doc):
    shard = lax.axis_index("seq")
    head = lax.axis_index("head").astype(jnp.int32)[None]
    row_count = queries.shape[0]
    half = out_grad.shape[1] // 2

    docs_here = lax.dynamic_slice_in_dim(query_doc, shard * row_count, row_count)
    slots = jnp.arange(N_SEQ, dtype=jnp.int32)[:, None]
    mine = docs_here[None, :] // DPS == slots
    rows = jnp.arange(row_count, dtype=jnp.int32)
    row_start = jnp.min(jnp.where(mine, rows[None, :], row_count - 1), axis=1)
    row_span = jnp.sum(mine.astype(jnp.int32), axis=1)
    got_q = to_all(pack_queries(row_start, row_span, queries))

    first = gather(out_grad[:, :half], along_x, along_y)
    second = gather(out_grad[:, half:], along_y, along_x)

    my_docs = shard * DPS + jnp.arange(DPS, dtype=jnp.int32)
    all_rows = jnp.arange(query_doc.shape[0], dtype=jnp.int32)
    source = jnp.max(jnp.where(query_doc[None, :] == my_docs[:, None], all_rows[None, :], 0), axis=1) // row_count
    local_blocks = enc_keys.shape[0] // BLOCK
    blocks_here = lax.dynamic_slice_in_dim(block_doc, shard * local_blocks, local_blocks)
    start = jnp.sum((blocks_here[None, :] < my_docs[:, None]).astype(jnp.int32), axis=1)
    count = jnp.sum((blocks_here[None, :] == my_docs[:, None]).astype(jnp.int32), axis=1)

    attended, weights = forward(source, start, count, got_q, enc_keys, enc_values)
    home = to_all(attended)
    got_g = to_all(attention_grads(row_start, row_span, head, out_proj, first, second))

    m_first, m_second, even, odd = mixed_parts(row_start, row_span, head, home, out_proj, first, second)
    mixed = jnp.concatenate(
        [scatter_sum(m_first, along_y, along_x), scatter_sum(m_second, along_x, along_y)],
        axis=1,
    )

    core = shard % 2
    swap = [(s, s ^ 1) for s in range(N_SEQ)]
    theirs = jnp.where(core == 0, odd, even).astype(jnp.bfloat16)
    other = lax.ppermute(theirs, "seq", swap)
    pair = (jnp.where(core == 0, even, odd) + other.astype(jnp.float32)).astype(jnp.bfloat16)
    chips = N_SEQ // 2
    turned = lax.dynamic_slice_in_dim(jnp.concatenate([pair, pair], axis=0), shard // 2, chips)
    terms = [turned[0]] + [shift(turned[k], along_z, k) for k in range(1, chips)]
    grad_wo = terms[0].astype(jnp.float32)
    for term in terms[1:]:
        grad_wo = grad_wo + term.astype(jnp.float32)

    grads_q, grad_k, grad_v = backward(
        source, start, count, got_q, got_g, attended, weights, enc_keys, enc_values
    )
    grad_q = unpack_grads(row_start, row_span, to_all(grads_q), row_count)
    return (mixed, grad_q, grad_k, grad_v, grad_wo)


def solution(mesh):
    placed = (
        P("seq", "head"),
        P("seq", "head"),
        P("seq", "head"),
        P("head", None),
        P(("seq", "head"), None),
        P(),
        P(),
    )
    return jax.shard_map(
        work,
        mesh=mesh,
        in_specs=placed,
        out_specs=(
            P(("seq", "head"), None),
            P("seq", "head"),
            P("seq", "head"),
            P("seq", "head"),
            P("head", "seq"),
        ),
        check_vma=False,
    )
```

```python
import jax
import jax.numpy as jnp
from jax import lax
from jax.experimental import pallas as pl
from jax.experimental.pallas import tpu as pltpu
from jax.sharding import PartitionSpec as P


BLOCK = 128
DPS = 8
SLOT = 144
TILE = 16
WINDOW = SLOT + TILE
CAP = 3
MASKED = -1e30
N_SEQ = 16
SIDE = 4
LANE_SPLIT = 64
SCALE = 0.125

VMEM = pltpu.MemorySpace.VMEM
SMEM = pltpu.MemorySpace.SMEM
HBM = pltpu.MemorySpace.HBM
LIMIT = pltpu.CompilerParams(vmem_limit_bytes=20 << 20)


def vmem_specs(count):
    return [pl.BlockSpec(memory_space=VMEM)] * count


def smem_specs(count):
    return [pl.BlockSpec(memory_space=SMEM)] * count


def dot(a, b, dims):
    return lax.dot_general(a, b, (dims, ((), ())), preferred_element_type=jnp.float32)


def select(equal):
    return jnp.where(equal, 1.0, 0.0).astype(jnp.bfloat16)


def window(start_ref, slot, row_count):
    start = start_ref[slot]
    base = pl.multiple_of(jnp.minimum(start // TILE * TILE, row_count - WINDOW), TILE)
    return pl.ds(base, WINDOW), start - base


def pack_rows(start_ref, count_ref, rows_ref, out_ref):
    lane = lax.broadcasted_iota(jnp.int32, (SLOT, WINDOW), 1)
    row = lax.broadcasted_iota(jnp.int32, (SLOT, WINDOW), 0)
    ahead = lane - row

    def step(slot, carry):
        span, skip = window(start_ref, slot, rows_ref.shape[0])
        chosen = select((ahead == skip) & (row < count_ref[slot]))
        out_ref[slot] = dot(chosen, rows_ref[span, :], ((1,), (0,))).astype(jnp.bfloat16)
        return carry

    lax.fori_loop(0, N_SEQ, step, 0, unroll=4)


def unpack_rows(start_ref, count_ref, packed_ref, sum_ref):
    lane = lax.broadcasted_iota(jnp.int32, (WINDOW, SLOT), 1)
    row = lax.broadcasted_iota(jnp.int32, (WINDOW, SLOT), 0)
    ahead = row - lane
    sum_ref[...] = jnp.zeros(sum_ref.shape, sum_ref.dtype)

    def step(slot, carry):
        span, skip = window(start_ref, slot, sum_ref.shape[0])
        chosen = select((ahead == skip) & (lane < count_ref[slot]))
        sum_ref[span, :] += dot(chosen, packed_ref[slot], ((1,), (0,)))
        return carry

    lax.fori_loop(0, N_SEQ, step, 0, unroll=4)


def block_rows(head_ref, behind_x, behind_y, unit):
    x, y = head_ref[0] // SIDE, head_ref[0] % SIDE
    block = (x + SIDE - behind_x) % SIDE * SIDE + (y + SIDE - behind_y) % SIDE
    return pl.ds(pl.multiple_of(block * unit, TILE), unit)


def pack_queries(start, count, queries):
    return pl.pallas_call(
        pack_rows,
        out_shape=jax.ShapeDtypeStruct((N_SEQ, SLOT, queries.shape[1]), jnp.bfloat16),
        in_specs=smem_specs(2) + vmem_specs(1),
        out_specs=pl.BlockSpec(memory_space=VMEM),
        compiler_params=LIMIT,
        name="pack_queries",
    )(start, count, queries)


def unpack_kernel(start_ref, count_ref, packed_ref, out_ref, sum_ref):
    unpack_rows(start_ref, count_ref, packed_ref, sum_ref)
    out_ref[...] = sum_ref[...].astype(jnp.bfloat16)


def unpack_grads(start, count, packed, row_count):
    shape = (row_count, packed.shape[2])
    return pl.pallas_call(
        unpack_kernel,
        out_shape=jax.ShapeDtypeStruct(shape, jnp.bfloat16),
        in_specs=smem_specs(2) + vmem_specs(1),
        out_specs=pl.BlockSpec(memory_space=VMEM),
        scratch_shapes=[pltpu.VMEM(shape, jnp.float32)],
        compiler_params=LIMIT,
        name="unpack_grads",
    )(start, count, packed)


def grad_kernel(start_ref, count_ref, head_ref, proj_ref, *refs):
    first, second, out_ref, rows_ref = refs[:SIDE], refs[SIDE : 2 * SIDE], refs[2 * SIDE], refs[2 * SIDE + 1]
    half = proj_ref.shape[1] // 2
    unit = rows_ref.shape[0] // (SIDE * SIDE)
    low = proj_ref[:, :half]
    high = proj_ref[:, half:]
    one = [dot(r[...], low, ((1,), (1,))) for r in first]
    two = [dot(r[...], high, ((1,), (1,))) for r in second]
    for a in range(SIDE):
        for b in range(SIDE):
            grads = one[a][b * unit : (b + 1) * unit] + two[b][a * unit : (a + 1) * unit]
            rows_ref[block_rows(head_ref, b, a, unit), :] = grads.astype(jnp.bfloat16)
    pack_rows(start_ref, count_ref, rows_ref, out_ref)


def attention_grads(start, count, head, out_proj, first, second):
    inner = out_proj.shape[0]
    row_count = SIDE * first[0].shape[0]
    return pl.pallas_call(
        grad_kernel,
        out_shape=jax.ShapeDtypeStruct((N_SEQ, SLOT, inner), jnp.bfloat16),
        in_specs=smem_specs(3) + vmem_specs(1 + 2 * SIDE),
        out_specs=pl.BlockSpec(memory_space=VMEM),
        scratch_shapes=[pltpu.VMEM((row_count, inner), jnp.bfloat16)],
        compiler_params=LIMIT,
        name="attention_grads",
    )(start, count, head, out_proj, *first, *second)


def two_heads(rows):
    low = lax.broadcasted_iota(jnp.int32, rows.shape, 1) < LANE_SPLIT
    zero = jnp.zeros_like(rows)
    return jnp.concatenate([jnp.where(low, rows, zero), jnp.where(low, zero, rows)], axis=0)


def one_row(stacked):
    half = stacked.shape[0] // 2
    low = lax.broadcasted_iota(jnp.int32, (half, stacked.shape[1]), 1) < LANE_SPLIT
    return jnp.where(low, stacked[:half], stacked[half:])


def document(refs, doc, block_total):
    source_ref, start_ref, count_ref = refs
    start = start_ref[doc]
    base = jnp.minimum(start, block_total - CAP)
    return source_ref[doc], base, start - base, count_ref[doc]


def forward_kernel(source_ref, start_ref, count_ref, q_ref, k_ref, v_ref, att_ref, w_ref, kept_ref, sems):
    att_ref[...] = jnp.zeros(att_ref.shape, att_ref.dtype)
    refs = (source_ref, start_ref, count_ref)
    lane = lax.broadcasted_iota(jnp.int32, (1, CAP * BLOCK), 1)
    copies = []
    for doc in range(DPS):
        source, base, skip, count = document(refs, doc, k_ref.shape[0] // BLOCK)
        tokens = pl.ds(pl.multiple_of(base * BLOCK, BLOCK), CAP * BLOCK)
        admitted = (lane >= skip * BLOCK) & (lane < (skip + count) * BLOCK)
        queries = two_heads(q_ref[source])
        scores = dot(queries, k_ref[tokens, :], ((1,), (1,))) * SCALE
        scores = jnp.where(admitted, scores, MASKED)
        top = jnp.max(scores, axis=1, keepdims=True)
        terms = jnp.exp(scores - top)
        scale = 1.0 / jnp.sum(terms, axis=1, keepdims=True)
        weights = (terms * scale).astype(jnp.bfloat16)
        kept_ref[doc] = weights
        copies.append(pltpu.make_async_copy(kept_ref.at[doc], w_ref.at[doc], sems.at[doc]))
        copies[-1].start()
        mixed = dot(weights, v_ref[tokens, :], ((1,), (0,)))
        att_ref[source] = one_row(mixed).astype(jnp.bfloat16)
    for copy in copies:
        copy.wait()


def forward(source, start, count, got_q, keys, values):
    weights = (DPS, 2 * SLOT, CAP * BLOCK)
    return pl.pallas_call(
        forward_kernel,
        out_shape=(jax.ShapeDtypeStruct(got_q.shape, jnp.bfloat16), HBM(weights, jnp.bfloat16)),
        in_specs=smem_specs(3) + vmem_specs(3),
        out_specs=(*vmem_specs(1), pl.BlockSpec(memory_space=HBM)),
        scratch_shapes=[pltpu.VMEM(weights, jnp.bfloat16), pltpu.SemaphoreType.DMA((DPS,))],
        compiler_params=LIMIT,
        name="forward",
    )(source, start, count, got_q, keys, values)


def backward_kernel(
    source_ref, start_ref, count_ref, q_ref, g_ref, att_ref, w_ref, k_ref, v_ref, dq_ref, dk_ref, dv_ref
):
    dq_ref[...] = jnp.zeros(dq_ref.shape, dq_ref.dtype)
    refs = (source_ref, start_ref, count_ref)
    for doc in range(DPS):
        source, base, skip, _ = document(refs, doc, k_ref.shape[0] // BLOCK)
        tokens = pl.ds(pl.multiple_of(base * BLOCK, BLOCK), CAP * BLOCK)
        queries = two_heads(q_ref[source])
        grads = two_heads(g_ref[source])
        attended = att_ref[source].astype(jnp.float32)
        both = jnp.concatenate([attended, attended], axis=0)
        delta = jnp.sum(grads.astype(jnp.float32) * both, axis=1, keepdims=True)
        weights = w_ref[doc]
        dprobs = dot(grads, v_ref[tokens, :], ((1,), (1,)))
        dscores = (weights.astype(jnp.float32) * (dprobs - delta)).astype(jnp.bfloat16)
        dq = dot(dscores, k_ref[tokens, :], ((1,), (0,)))
        dq_ref[source] = (one_row(dq) * SCALE).astype(jnp.bfloat16)
        dk = (dot(dscores, queries, ((0,), (0,))) * SCALE).astype(jnp.bfloat16)
        dv = dot(weights, grads, ((0,), (0,))).astype(jnp.bfloat16)
        for part in range(CAP):
            rows = pl.ds(pl.multiple_of((base + part) * BLOCK, BLOCK), BLOCK)
            span = slice(part * BLOCK, (part + 1) * BLOCK)
            if part == CAP - 1:
                dk_ref[rows, :] = dk[span]
                dv_ref[rows, :] = dv[span]
            else:
                keep = skip > part
                dk_ref[rows, :] = jnp.where(keep, dk_ref[rows, :], dk[span])
                dv_ref[rows, :] = jnp.where(keep, dv_ref[rows, :], dv[span])


def backward(source, start, count, got_q, got_g, attended, weights, keys, values):
    return pl.pallas_call(
        backward_kernel,
        out_shape=(
            jax.ShapeDtypeStruct(got_q.shape, jnp.bfloat16),
            jax.ShapeDtypeStruct(keys.shape, jnp.bfloat16),
            jax.ShapeDtypeStruct(values.shape, jnp.bfloat16),
        ),
        in_specs=smem_specs(3) + vmem_specs(6),
        out_specs=tuple(vmem_specs(3)),
        compiler_params=LIMIT,
        name="backward",
    )(source, start, count, got_q, got_g, attended, weights, keys, values)


def mixed_kernel(start_ref, count_ref, head_ref, packed_ref, proj_ref, *refs):
    first, second = refs[:SIDE], refs[SIDE : 2 * SIDE]
    outs = refs[2 * SIDE : 4 * SIDE]
    even_ref, odd_ref, sum_ref, sent_ref, weight_ref, sems = refs[4 * SIDE :]
    unpack_rows(start_ref, count_ref, packed_ref, sum_ref)
    unit = sum_ref.shape[0] // (SIDE * SIDE)
    half = proj_ref.shape[1] // 2
    blocks = [
        [sum_ref[block_rows(head_ref, b, a, unit), :].astype(jnp.bfloat16) for b in range(SIDE)]
        for a in range(SIDE)
    ]
    rows = [jnp.concatenate(blocks[a], axis=0) for a in range(SIDE)]
    rows_two = [jnp.concatenate([blocks[a][b] for a in range(SIDE)], axis=0) for b in range(SIDE)]
    copies = []
    for h, part in enumerate((rows, rows_two)):
        cols = slice(h * half, (h + 1) * half)
        for p in (1, 3, 2, 0):
            place = h * SIDE + p
            sent_ref[place] = dot(part[p], proj_ref[:, cols], ((1,), (0,))).astype(jnp.bfloat16)
            copies.append(pltpu.make_async_copy(sent_ref.at[place], outs[place], sems.at[place]))
            copies[-1].start()
    sums = []
    for part, ins in ((rows, first), (rows_two, second)):
        term = None
        for p in range(SIDE):
            more = dot(part[p], ins[p][...], ((0,), (0,)))
            term = more if term is None else term + more
        sums.append(term)
    per_half = half // BLOCK
    for h in range(2):
        for c in range(per_half):
            chunk = h * per_half + c
            weight_ref[chunk % 2, chunk // 2] = sums[h][:, c * BLOCK : (c + 1) * BLOCK]
    for c, out_ref in enumerate((even_ref, odd_ref)):
        copies.append(pltpu.make_async_copy(weight_ref.at[c], out_ref, sems.at[2 * SIDE + c]))
        copies[-1].start()
    for copy in copies:
        copy.wait()


def mixed_parts(start, count, head, packed, out_proj, first, second):
    inner, width = out_proj.shape
    row_count = SIDE * first[0].shape[0]
    part = HBM(first[0].shape, jnp.bfloat16)
    sums = HBM((width // BLOCK // 2, inner, BLOCK), jnp.float32)
    outs = pl.pallas_call(
        mixed_kernel,
        out_shape=(part,) * (2 * SIDE) + (sums,) * 2,
        in_specs=smem_specs(3) + vmem_specs(2 + 2 * SIDE),
        out_specs=tuple([pl.BlockSpec(memory_space=HBM)] * (2 * SIDE + 2)),
        scratch_shapes=[
            pltpu.VMEM((row_count, inner), jnp.float32),
            pltpu.VMEM((2 * SIDE, *first[0].shape), jnp.bfloat16),
            pltpu.VMEM((2, width // BLOCK // 2, inner, BLOCK), jnp.float32),
            pltpu.SemaphoreType.DMA((2 * SIDE + 2,)),
        ],
        compiler_params=LIMIT,
        name="mixed_parts",
    )(start, count, head, packed, out_proj, *first, *second)
    return outs[:SIDE], outs[SIDE : 2 * SIDE], outs[2 * SIDE], outs[2 * SIDE + 1]


def along_x(value, k):
    perm = [(x * SIDE + y, (x + k) % SIDE * SIDE + y) for x in range(SIDE) for y in range(SIDE)]
    return lax.ppermute(value, "head", perm)


def along_y(value, k):
    perm = [(x * SIDE + y, x * SIDE + (y + k) % SIDE) for x in range(SIDE) for y in range(SIDE)]
    return lax.ppermute(value, "head", perm)


def halve(low, high, side, distance):
    swap = [(s, s ^ distance) for s in range(N_SEQ)]
    theirs = jnp.where(side == 0, high, low).astype(jnp.bfloat16)
    other = lax.ppermute(theirs, "seq", swap)
    return jnp.where(side == 0, low, high) + other.astype(jnp.float32)


def shift(value, move, k):
    return move(value, k)


def gather(value, one, two):
    rows = jnp.concatenate([value] + [shift(value, one, k) for k in range(1, SIDE)], axis=0)
    return [rows] + [shift(rows, two, k) for k in range(1, SIDE)]


def total(parts):
    out = parts[0].astype(jnp.float32)
    for part in parts[1:]:
        out = out + part.astype(jnp.float32)
    return out.astype(jnp.bfloat16)


def scatter_sum(parts, one, two):
    terms = [parts[0]] + [shift(parts[k], one, SIDE - k) for k in range(1, SIDE)]
    rows = total(terms)
    unit = rows.shape[0] // SIDE
    terms = [rows[:unit]] + [shift(rows[k * unit : (k + 1) * unit], two, SIDE - k) for k in range(1, SIDE)]
    return total(terms)


def to_all(value):
    return lax.all_to_all(value, "seq", split_axis=0, concat_axis=0, tiled=True)


def work(queries, enc_keys, enc_values, out_proj, out_grad, block_doc, query_doc):
    shard = lax.axis_index("seq")
    head = lax.axis_index("head").astype(jnp.int32)[None]
    row_count = queries.shape[0]
    half = out_grad.shape[1] // 2

    docs_here = lax.dynamic_slice_in_dim(query_doc, shard * row_count, row_count)
    slots = jnp.arange(N_SEQ, dtype=jnp.int32)[:, None]
    mine = docs_here[None, :] // DPS == slots
    rows = jnp.arange(row_count, dtype=jnp.int32)
    row_start = jnp.min(jnp.where(mine, rows[None, :], row_count - 1), axis=1)
    row_span = jnp.sum(mine.astype(jnp.int32), axis=1)
    got_q = to_all(pack_queries(row_start, row_span, queries))

    first = gather(out_grad[:, :half], along_x, along_y)
    second = gather(out_grad[:, half:], along_y, along_x)

    my_docs = shard * DPS + jnp.arange(DPS, dtype=jnp.int32)
    all_rows = jnp.arange(query_doc.shape[0], dtype=jnp.int32)
    source = jnp.max(jnp.where(query_doc[None, :] == my_docs[:, None], all_rows[None, :], 0), axis=1) // row_count
    local_blocks = enc_keys.shape[0] // BLOCK
    blocks_here = lax.dynamic_slice_in_dim(block_doc, shard * local_blocks, local_blocks)
    start = jnp.sum((blocks_here[None, :] < my_docs[:, None]).astype(jnp.int32), axis=1)
    count = jnp.sum((blocks_here[None, :] == my_docs[:, None]).astype(jnp.int32), axis=1)

    attended, weights = forward(source, start, count, got_q, enc_keys, enc_values)
    home = to_all(attended)
    got_g = to_all(attention_grads(row_start, row_span, head, out_proj, first, second))

    m_first, m_second, even, odd = mixed_parts(row_start, row_span, head, home, out_proj, first, second)
    mixed = jnp.concatenate(
        [scatter_sum(m_first, along_y, along_x), scatter_sum(m_second, along_x, along_y)],
        axis=1,
    )

    core = shard % 2
    chip = shard // 2
    grad_wo = halve(even, odd, core, 1)
    for bit in range(3):
        halves = grad_wo.reshape(-1, 2, *grad_wo.shape[1:])
        grad_wo = halve(halves[:, 0], halves[:, 1], (chip >> bit) & 1, 2 << bit)
    grad_wo = grad_wo[0]

    grads_q, grad_k, grad_v = backward(
        source, start, count, got_q, got_g, attended, weights, enc_keys, enc_values
    )
    grad_q = unpack_grads(row_start, row_span, to_all(grads_q), row_count)
    return (mixed, grad_q, grad_k, grad_v, grad_wo)


def solution(mesh):
    placed = (
        P("seq", "head"),
        P("seq", "head"),
        P("seq", "head"),
        P("head", None),
        P(("seq", "head"), None),
        P(),
        P(),
    )
    return jax.shard_map(
        work,
        mesh=mesh,
        in_specs=placed,
        out_specs=(
            P(("seq", "head"), None),
            P("seq", "head"),
            P("seq", "head"),
            P("seq", "head"),
            P("head", "seq"),
        ),
        check_vma=False,
    )
```

```python
import jax
import jax.numpy as jnp
from jax import lax
from jax.experimental import pallas as pl
from jax.experimental.pallas import tpu as pltpu
from jax.sharding import PartitionSpec as P


BLOCK = 128
DPS = 8
SLOT = 144
TILE = 16
WINDOW = SLOT + TILE
CAP = 3
MASKED = -1e30
N_SEQ = 16
SIDE = 4
LANE_SPLIT = 64
SCALE = 0.125

VMEM = pltpu.MemorySpace.VMEM
SMEM = pltpu.MemorySpace.SMEM
HBM = pltpu.MemorySpace.HBM
LIMIT = pltpu.CompilerParams(vmem_limit_bytes=20 << 20)


def vmem_specs(count):
    return [pl.BlockSpec(memory_space=VMEM)] * count


def smem_specs(count):
    return [pl.BlockSpec(memory_space=SMEM)] * count


def dot(a, b, dims):
    return lax.dot_general(a, b, (dims, ((), ())), preferred_element_type=jnp.float32)


def select(equal):
    return jnp.where(equal, 1.0, 0.0).astype(jnp.bfloat16)


def window(start_ref, slot, row_count):
    start = start_ref[slot]
    base = pl.multiple_of(jnp.minimum(start // TILE * TILE, row_count - WINDOW), TILE)
    return pl.ds(base, WINDOW), start - base


def pack_rows(start_ref, count_ref, rows_ref, out_ref):
    lane = lax.broadcasted_iota(jnp.int32, (SLOT, WINDOW), 1)
    row = lax.broadcasted_iota(jnp.int32, (SLOT, WINDOW), 0)
    ahead = lane - row

    def step(slot, carry):
        span, skip = window(start_ref, slot, rows_ref.shape[0])
        chosen = select((ahead == skip) & (row < count_ref[slot]))
        out_ref[slot] = dot(chosen, rows_ref[span, :], ((1,), (0,))).astype(jnp.bfloat16)
        return carry

    lax.fori_loop(0, N_SEQ, step, 0, unroll=4)


def unpack_rows(start_ref, count_ref, packed_ref, sum_ref):
    lane = lax.broadcasted_iota(jnp.int32, (WINDOW, SLOT), 1)
    row = lax.broadcasted_iota(jnp.int32, (WINDOW, SLOT), 0)
    ahead = row - lane
    sum_ref[...] = jnp.zeros(sum_ref.shape, sum_ref.dtype)

    def step(slot, carry):
        span, skip = window(start_ref, slot, sum_ref.shape[0])
        chosen = select((ahead == skip) & (lane < count_ref[slot]))
        sum_ref[span, :] += dot(chosen, packed_ref[slot], ((1,), (0,)))
        return carry

    lax.fori_loop(0, N_SEQ, step, 0, unroll=4)


def block_rows(head_ref, behind_x, behind_y, unit):
    x, y = head_ref[0] // SIDE, head_ref[0] % SIDE
    block = (x + SIDE - behind_x) % SIDE * SIDE + (y + SIDE - behind_y) % SIDE
    return pl.ds(pl.multiple_of(block * unit, TILE), unit)


def pack_queries(start, count, queries):
    return pl.pallas_call(
        pack_rows,
        out_shape=jax.ShapeDtypeStruct((N_SEQ, SLOT, queries.shape[1]), jnp.bfloat16),
        in_specs=smem_specs(2) + vmem_specs(1),
        out_specs=pl.BlockSpec(memory_space=VMEM),
        compiler_params=LIMIT,
        name="pack_queries",
    )(start, count, queries)


def unpack_kernel(start_ref, count_ref, packed_ref, out_ref, sum_ref):
    unpack_rows(start_ref, count_ref, packed_ref, sum_ref)
    out_ref[...] = sum_ref[...].astype(jnp.bfloat16)


def unpack_grads(start, count, packed, row_count):
    shape = (row_count, packed.shape[2])
    return pl.pallas_call(
        unpack_kernel,
        out_shape=jax.ShapeDtypeStruct(shape, jnp.bfloat16),
        in_specs=smem_specs(2) + vmem_specs(1),
        out_specs=pl.BlockSpec(memory_space=VMEM),
        scratch_shapes=[pltpu.VMEM(shape, jnp.float32)],
        compiler_params=LIMIT,
        name="unpack_grads",
    )(start, count, packed)


def grad_kernel(start_ref, count_ref, head_ref, proj_ref, *refs):
    first, second, out_ref, rows_ref = refs[:SIDE], refs[SIDE : 2 * SIDE], refs[2 * SIDE], refs[2 * SIDE + 1]
    half = proj_ref.shape[1] // 2
    unit = rows_ref.shape[0] // (SIDE * SIDE)
    low = proj_ref[:, :half]
    high = proj_ref[:, half:]
    one = [dot(r[...], low, ((1,), (1,))) for r in first]
    two = [dot(r[...], high, ((1,), (1,))) for r in second]
    for a in range(SIDE):
        for b in range(SIDE):
            grads = one[a][b * unit : (b + 1) * unit] + two[b][a * unit : (a + 1) * unit]
            rows_ref[block_rows(head_ref, b, a, unit), :] = grads.astype(jnp.bfloat16)
    pack_rows(start_ref, count_ref, rows_ref, out_ref)


def attention_grads(start, count, head, out_proj, first, second):
    inner = out_proj.shape[0]
    row_count = SIDE * first[0].shape[0]
    return pl.pallas_call(
        grad_kernel,
        out_shape=jax.ShapeDtypeStruct((N_SEQ, SLOT, inner), jnp.bfloat16),
        in_specs=smem_specs(3) + vmem_specs(1 + 2 * SIDE),
        out_specs=pl.BlockSpec(memory_space=VMEM),
        scratch_shapes=[pltpu.VMEM((row_count, inner), jnp.bfloat16)],
        compiler_params=LIMIT,
        name="attention_grads",
    )(start, count, head, out_proj, *first, *second)


def two_heads(rows):
    low = lax.broadcasted_iota(jnp.int32, rows.shape, 1) < LANE_SPLIT
    zero = jnp.zeros_like(rows)
    return jnp.concatenate([jnp.where(low, rows, zero), jnp.where(low, zero, rows)], axis=0)


def one_row(stacked):
    half = stacked.shape[0] // 2
    low = lax.broadcasted_iota(jnp.int32, (half, stacked.shape[1]), 1) < LANE_SPLIT
    return jnp.where(low, stacked[:half], stacked[half:])


def document(refs, doc, block_total):
    source_ref, start_ref, count_ref = refs
    start = start_ref[doc]
    base = jnp.minimum(start, block_total - CAP)
    return source_ref[doc], base, start - base, count_ref[doc]


def forward_kernel(source_ref, start_ref, count_ref, q_ref, k_ref, v_ref, att_ref, out_ref, w_ref, sems):
    att_ref[...] = jnp.zeros(att_ref.shape, att_ref.dtype)
    refs = (source_ref, start_ref, count_ref)
    lane = lax.broadcasted_iota(jnp.int32, (1, CAP * BLOCK), 1)
    copies = []
    for doc in range(DPS):
        source, base, skip, count = document(refs, doc, k_ref.shape[0] // BLOCK)
        tokens = pl.ds(pl.multiple_of(base * BLOCK, BLOCK), CAP * BLOCK)
        admitted = (lane >= skip * BLOCK) & (lane < (skip + count) * BLOCK)
        queries = two_heads(q_ref[source] * SCALE)
        scores = dot(queries, k_ref[tokens, :], ((1,), (1,)))
        scores = jnp.where(admitted, scores, MASKED)
        top = jnp.max(scores, axis=1, keepdims=True)
        terms = jnp.exp(scores - top)
        scale = 1.0 / jnp.sum(terms, axis=1, keepdims=True)
        weights = (terms * scale).astype(jnp.bfloat16)
        for part in range(CAP):
            mine = weights[:, part * BLOCK : (part + 1) * BLOCK]
            if part < CAP - 1:
                mine = jnp.where(skip > part, w_ref[base + part], mine)
            w_ref[base + part] = mine
        copies.append(pltpu.make_async_copy(w_ref.at[doc], out_ref.at[doc], sems.at[doc]))
        copies[-1].start()
        mixed = dot(weights, v_ref[tokens, :], ((1,), (0,)))
        att_ref[source] = one_row(mixed).astype(jnp.bfloat16)
    rest = slice(DPS, w_ref.shape[0])
    copies.append(pltpu.make_async_copy(w_ref.at[rest], out_ref.at[rest], sems.at[DPS]))
    copies[-1].start()
    for copy in copies:
        copy.wait()


def forward(source, start, count, got_q, keys, values):
    weights = (keys.shape[0] // BLOCK, 2 * SLOT, BLOCK)
    return pl.pallas_call(
        forward_kernel,
        out_shape=(
            jax.ShapeDtypeStruct(got_q.shape, jnp.bfloat16),
            HBM(weights, jnp.bfloat16),
        ),
        in_specs=smem_specs(3) + vmem_specs(3),
        out_specs=(*vmem_specs(1), pl.BlockSpec(memory_space=HBM)),
        scratch_shapes=[pltpu.VMEM(weights, jnp.bfloat16), pltpu.SemaphoreType.DMA((DPS + 1,))],
        compiler_params=LIMIT,
        name="forward",
    )(source, start, count, got_q, keys, values)


def backward_kernel(
    source_ref, owner_ref, q_ref, g_ref, att_ref, kept_ref, k_ref, v_ref,
    dq_ref, dk_ref, dv_ref, w_ref, sem, queries_ref, grads_ref, delta_ref, sum_ref
):
    fetch = pltpu.make_async_copy(kept_ref, w_ref, sem)
    fetch.start()
    dq_ref[...] = jnp.zeros(dq_ref.shape, dq_ref.dtype)
    for doc in range(DPS):
        source = source_ref[doc]
        queries_ref[doc] = two_heads(q_ref[source])
        grads = two_heads(g_ref[source])
        grads_ref[doc] = grads
        attended = att_ref[source].astype(jnp.float32)
        both = jnp.concatenate([attended, attended], axis=0)
        delta_ref[doc] = jnp.sum(grads.astype(jnp.float32) * both, axis=1, keepdims=True)
        sum_ref[doc] = jnp.zeros(sum_ref.shape[1:], sum_ref.dtype)
    fetch.wait()
    for block in range(w_ref.shape[0]):
        doc = owner_ref[block]
        tokens = slice(block * BLOCK, (block + 1) * BLOCK)
        grads = grads_ref[doc]
        weights = w_ref[block]
        dprobs = dot(grads, v_ref[tokens, :], ((1,), (1,)))
        dscores = (weights.astype(jnp.float32) * (dprobs - delta_ref[doc])).astype(jnp.bfloat16)
        sum_ref[doc] += dot(dscores, k_ref[tokens, :], ((1,), (0,)))
        dk_ref[tokens, :] = (dot(dscores, queries_ref[doc], ((0,), (0,))) * SCALE).astype(jnp.bfloat16)
        dv_ref[tokens, :] = dot(weights, grads, ((0,), (0,))).astype(jnp.bfloat16)
    for doc in range(DPS):
        dq_ref[source_ref[doc]] = (one_row(sum_ref[doc]) * SCALE).astype(jnp.bfloat16)


def backward(source, owner, got_q, got_g, attended, weights, keys, values):
    stacked = (DPS, 2 * SLOT, got_q.shape[2])
    return pl.pallas_call(
        backward_kernel,
        out_shape=(
            jax.ShapeDtypeStruct(got_q.shape, jnp.bfloat16),
            jax.ShapeDtypeStruct(keys.shape, jnp.bfloat16),
            jax.ShapeDtypeStruct(values.shape, jnp.bfloat16),
        ),
        in_specs=smem_specs(2) + vmem_specs(3) + [pl.BlockSpec(memory_space=HBM)] + vmem_specs(2),
        out_specs=tuple(vmem_specs(3)),
        scratch_shapes=[
            pltpu.VMEM(weights.shape, jnp.bfloat16),
            pltpu.SemaphoreType.DMA,
            pltpu.VMEM(stacked, jnp.bfloat16),
            pltpu.VMEM(stacked, jnp.bfloat16),
            pltpu.VMEM((DPS, 2 * SLOT, 1), jnp.float32),
            pltpu.VMEM(stacked, jnp.float32),
        ],
        compiler_params=LIMIT,
        name="backward",
    )(source, owner, got_q, got_g, attended, weights, keys, values)


def mixed_kernel(start_ref, count_ref, head_ref, core_ref, packed_ref, proj_ref, *refs):
    first, second = refs[:SIDE], refs[SIDE : 2 * SIDE]
    outs = refs[2 * SIDE : 4 * SIDE]
    mine_ref, theirs_ref, sum_ref, sent_ref, weight_ref, other_ref, sems = refs[4 * SIDE :]
    unpack_rows(start_ref, count_ref, packed_ref, sum_ref)
    unit = sum_ref.shape[0] // (SIDE * SIDE)
    half = proj_ref.shape[1] // 2
    blocks = [
        [sum_ref[block_rows(head_ref, b, a, unit), :].astype(jnp.bfloat16) for b in range(SIDE)]
        for a in range(SIDE)
    ]
    rows = [jnp.concatenate(blocks[a], axis=0) for a in range(SIDE)]
    rows_two = [jnp.concatenate([blocks[a][b] for a in range(SIDE)], axis=0) for b in range(SIDE)]
    copies = []
    for h, part in enumerate((rows, rows_two)):
        cols = slice(h * half, (h + 1) * half)
        for p in (1, 3, 2, 0):
            place = h * SIDE + p
            sent_ref[place] = dot(part[p], proj_ref[:, cols], ((1,), (0,))).astype(jnp.bfloat16)
            copies.append(pltpu.make_async_copy(sent_ref.at[place], outs[place], sems.at[place]))
            copies[-1].start()
    sums = []
    for part, ins in ((rows, first), (rows_two, second)):
        term = None
        for p in range(SIDE):
            more = dot(part[p], ins[p][...], ((0,), (0,)))
            term = more if term is None else term + more
        sums.append(term)
    per_half = half // BLOCK
    for h in range(2):
        for c in range(per_half):
            chunk = h * per_half + c
            weight_ref[chunk % 2, chunk // 2] = sums[h][:, c * BLOCK : (c + 1) * BLOCK]
    core = core_ref[0]
    other_ref[...] = weight_ref[1 - core].astype(jnp.bfloat16)
    copies.append(pltpu.make_async_copy(other_ref, theirs_ref, sems.at[2 * SIDE]))
    copies[-1].start()
    copies.append(pltpu.make_async_copy(weight_ref.at[core], mine_ref, sems.at[2 * SIDE + 1]))
    copies[-1].start()
    for copy in copies:
        copy.wait()


def mixed_parts(start, count, head, core, packed, out_proj, first, second):
    inner, width = out_proj.shape
    row_count = SIDE * first[0].shape[0]
    part = HBM(first[0].shape, jnp.bfloat16)
    chunks = (width // BLOCK // 2, inner, BLOCK)
    outs = pl.pallas_call(
        mixed_kernel,
        out_shape=(part,) * (2 * SIDE) + (HBM(chunks, jnp.float32), HBM(chunks, jnp.bfloat16)),
        in_specs=smem_specs(4) + vmem_specs(2 + 2 * SIDE),
        out_specs=tuple([pl.BlockSpec(memory_space=HBM)] * (2 * SIDE + 2)),
        scratch_shapes=[
            pltpu.VMEM((row_count, inner), jnp.float32),
            pltpu.VMEM((2 * SIDE, *first[0].shape), jnp.bfloat16),
            pltpu.VMEM((2, *chunks), jnp.float32),
            pltpu.VMEM(chunks, jnp.bfloat16),
            pltpu.SemaphoreType.DMA((2 * SIDE + 2,)),
        ],
        compiler_params=LIMIT,
        name="mixed_parts",
    )(start, count, head, core, packed, out_proj, *first, *second)
    return outs[:SIDE], outs[SIDE : 2 * SIDE], outs[2 * SIDE], outs[2 * SIDE + 1]


def along_x(value, k):
    perm = [(x * SIDE + y, (x + k) % SIDE * SIDE + y) for x in range(SIDE) for y in range(SIDE)]
    return lax.ppermute(value, "head", perm)


def along_y(value, k):
    perm = [(x * SIDE + y, x * SIDE + (y + k) % SIDE) for x in range(SIDE) for y in range(SIDE)]
    return lax.ppermute(value, "head", perm)


def add_other(mine, theirs, distance):
    swap = [(s, s ^ distance) for s in range(N_SEQ)]
    other = lax.ppermute(theirs, "seq", swap)
    return mine + other.astype(jnp.float32)


def halve(low, high, side, distance):
    theirs = jnp.where(side == 0, high, low).astype(jnp.bfloat16)
    return add_other(jnp.where(side == 0, low, high), theirs, distance)


def shift(value, move, k):
    return move(value, k)


def gather(value, one, two):
    rows = jnp.concatenate([value] + [shift(value, one, k) for k in range(1, SIDE)], axis=0)
    return [rows] + [shift(rows, two, k) for k in range(1, SIDE)]


def total(parts):
    out = parts[0].astype(jnp.float32)
    for part in parts[1:]:
        out = out + part.astype(jnp.float32)
    return out.astype(jnp.bfloat16)


def scatter_sum(parts, one, two):
    terms = [parts[0]] + [shift(parts[k], one, SIDE - k) for k in range(1, SIDE)]
    rows = total(terms)
    unit = rows.shape[0] // SIDE
    terms = [rows[:unit]] + [shift(rows[k * unit : (k + 1) * unit], two, SIDE - k) for k in range(1, SIDE)]
    return total(terms)


def to_all(value):
    return lax.all_to_all(value, "seq", split_axis=0, concat_axis=0, tiled=True)


def work(queries, enc_keys, enc_values, out_proj, out_grad, block_doc, query_doc):
    shard = lax.axis_index("seq")
    head = lax.axis_index("head").astype(jnp.int32)[None]
    row_count = queries.shape[0]
    half = out_grad.shape[1] // 2

    docs_here = lax.dynamic_slice_in_dim(query_doc, shard * row_count, row_count)
    slots = jnp.arange(N_SEQ, dtype=jnp.int32)[:, None]
    mine = docs_here[None, :] // DPS == slots
    rows = jnp.arange(row_count, dtype=jnp.int32)
    row_start = jnp.min(jnp.where(mine, rows[None, :], row_count - 1), axis=1)
    row_span = jnp.sum(mine.astype(jnp.int32), axis=1)
    got_q = to_all(pack_queries(row_start, row_span, queries))

    first = gather(out_grad[:, :half], along_x, along_y)
    second = gather(out_grad[:, half:], along_y, along_x)

    my_docs = shard * DPS + jnp.arange(DPS, dtype=jnp.int32)
    all_rows = jnp.arange(query_doc.shape[0], dtype=jnp.int32)
    source = jnp.max(jnp.where(query_doc[None, :] == my_docs[:, None], all_rows[None, :], 0), axis=1) // row_count
    local_blocks = enc_keys.shape[0] // BLOCK
    blocks_here = lax.dynamic_slice_in_dim(block_doc, shard * local_blocks, local_blocks)
    start = jnp.sum((blocks_here[None, :] < my_docs[:, None]).astype(jnp.int32), axis=1)
    count = jnp.sum((blocks_here[None, :] == my_docs[:, None]).astype(jnp.int32), axis=1)

    owner = blocks_here - shard * DPS

    attended, weights = forward(source, start, count, got_q, enc_keys, enc_values)
    home = to_all(attended)
    got_g = to_all(attention_grads(row_start, row_span, head, out_proj, first, second))

    core = shard % 2
    m_first, m_second, mine, theirs = mixed_parts(row_start, row_span, head, core[None], home, out_proj, first, second)
    mixed = jnp.concatenate(
        [scatter_sum(m_first, along_y, along_x), scatter_sum(m_second, along_x, along_y)],
        axis=1,
    )

    chip = shard // 2
    grad_wo = add_other(mine, theirs, 1)
    for bit in range(3):
        halves = grad_wo.reshape(-1, 2, *grad_wo.shape[1:])
        grad_wo = halve(halves[:, 0], halves[:, 1], (chip >> bit) & 1, 2 << bit)
    grad_wo = grad_wo[0]

    grads_q, grad_k, grad_v = backward(
        source, owner, got_q, got_g, attended, weights, enc_keys, enc_values
    )
    grad_q = unpack_grads(row_start, row_span, to_all(grads_q), row_count)
    return (mixed, grad_q, grad_k, grad_v, grad_wo)


def solution(mesh):
    placed = (
        P("seq", "head"),
        P("seq", "head"),
        P("seq", "head"),
        P("head", None),
        P(("seq", "head"), None),
        P(),
        P(),
    )
    return jax.shard_map(
        work,
        mesh=mesh,
        in_specs=placed,
        out_specs=(
            P(("seq", "head"), None),
            P("seq", "head"),
            P("seq", "head"),
            P("seq", "head"),
            P("head", "seq"),
        ),
        check_vma=False,
    )
```

```python
import jax
import jax.numpy as jnp
from jax import lax
from jax.experimental import pallas as pl
from jax.experimental.pallas import tpu as pltpu
from jax.sharding import PartitionSpec as P


BLOCK = 128
DPS = 8
SLOT = 144
TILE = 16
WINDOW = SLOT + TILE
CAP = 3
MASKED = -1e30
N_SEQ = 16
SIDE = 4
LANE_SPLIT = 64
SCALE = 0.125

VMEM = pltpu.MemorySpace.VMEM
SMEM = pltpu.MemorySpace.SMEM
HBM = pltpu.MemorySpace.HBM
LIMIT = pltpu.CompilerParams(vmem_limit_bytes=20 << 20)


def vmem_specs(count):
    return [pl.BlockSpec(memory_space=VMEM)] * count


def smem_specs(count):
    return [pl.BlockSpec(memory_space=SMEM)] * count


def dot(a, b, dims):
    return lax.dot_general(a, b, (dims, ((), ())), preferred_element_type=jnp.float32)


def select(equal):
    return jnp.where(equal, 1.0, 0.0).astype(jnp.bfloat16)


def window(start_ref, slot, row_count):
    start = start_ref[slot]
    base = pl.multiple_of(jnp.minimum(start // TILE * TILE, row_count - WINDOW), TILE)
    return pl.ds(base, WINDOW), start - base


def pack_rows(start_ref, count_ref, rows_ref, out_ref):
    lane = lax.broadcasted_iota(jnp.int32, (SLOT, WINDOW), 1)
    row = lax.broadcasted_iota(jnp.int32, (SLOT, WINDOW), 0)
    ahead = lane - row

    def step(slot, carry):
        span, skip = window(start_ref, slot, rows_ref.shape[0])
        chosen = select((ahead == skip) & (row < count_ref[slot]))
        out_ref[slot] = dot(chosen, rows_ref[span, :], ((1,), (0,))).astype(jnp.bfloat16)
        return carry

    lax.fori_loop(0, N_SEQ, step, 0, unroll=4)


def unpack_rows(start_ref, count_ref, packed_ref, sum_ref):
    lane = lax.broadcasted_iota(jnp.int32, (WINDOW, SLOT), 1)
    row = lax.broadcasted_iota(jnp.int32, (WINDOW, SLOT), 0)
    ahead = row - lane
    sum_ref[...] = jnp.zeros(sum_ref.shape, sum_ref.dtype)

    def step(slot, carry):
        span, skip = window(start_ref, slot, sum_ref.shape[0])
        chosen = select((ahead == skip) & (lane < count_ref[slot]))
        sum_ref[span, :] += dot(chosen, packed_ref[slot], ((1,), (0,)))
        return carry

    lax.fori_loop(0, N_SEQ, step, 0, unroll=4)


def block_rows(head_ref, behind_x, behind_y, unit):
    x, y = head_ref[0] // SIDE, head_ref[0] % SIDE
    block = (x + SIDE - behind_x) % SIDE * SIDE + (y + SIDE - behind_y) % SIDE
    return pl.ds(pl.multiple_of(block * unit, TILE), unit)


def pack_queries(start, count, queries):
    return pl.pallas_call(
        pack_rows,
        out_shape=jax.ShapeDtypeStruct((N_SEQ, SLOT, queries.shape[1]), jnp.bfloat16),
        in_specs=smem_specs(2) + vmem_specs(1),
        out_specs=pl.BlockSpec(memory_space=VMEM),
        compiler_params=LIMIT,
        name="pack_queries",
    )(start, count, queries)


def unpack_kernel(start_ref, count_ref, packed_ref, out_ref, sum_ref):
    unpack_rows(start_ref, count_ref, packed_ref, sum_ref)
    out_ref[...] = sum_ref[...].astype(jnp.bfloat16)


def unpack_grads(start, count, packed, row_count):
    shape = (row_count, packed.shape[2])
    return pl.pallas_call(
        unpack_kernel,
        out_shape=jax.ShapeDtypeStruct(shape, jnp.bfloat16),
        in_specs=smem_specs(2) + vmem_specs(1),
        out_specs=pl.BlockSpec(memory_space=VMEM),
        scratch_shapes=[pltpu.VMEM(shape, jnp.float32)],
        compiler_params=LIMIT,
        name="unpack_grads",
    )(start, count, packed)


def grad_kernel(start_ref, count_ref, head_ref, proj_ref, *refs):
    first, second, out_ref, rows_ref = refs[:SIDE], refs[SIDE : 2 * SIDE], refs[2 * SIDE], refs[2 * SIDE + 1]
    half = proj_ref.shape[1] // 2
    unit = rows_ref.shape[0] // (SIDE * SIDE)
    low = proj_ref[:, :half]
    high = proj_ref[:, half:]
    one = [dot(r[...], low, ((1,), (1,))) for r in first]
    two = [dot(r[...], high, ((1,), (1,))) for r in second]
    for a in range(SIDE):
        for b in range(SIDE):
            grads = one[a][b * unit : (b + 1) * unit] + two[b][a * unit : (a + 1) * unit]
            rows_ref[block_rows(head_ref, b, a, unit), :] = grads.astype(jnp.bfloat16)
    pack_rows(start_ref, count_ref, rows_ref, out_ref)


def attention_grads(start, count, head, out_proj, first, second):
    inner = out_proj.shape[0]
    row_count = SIDE * first[0].shape[0]
    return pl.pallas_call(
        grad_kernel,
        out_shape=jax.ShapeDtypeStruct((N_SEQ, SLOT, inner), jnp.bfloat16),
        in_specs=smem_specs(3) + vmem_specs(1 + 2 * SIDE),
        out_specs=pl.BlockSpec(memory_space=VMEM),
        scratch_shapes=[pltpu.VMEM((row_count, inner), jnp.bfloat16)],
        compiler_params=LIMIT,
        name="attention_grads",
    )(start, count, head, out_proj, *first, *second)


def two_heads(rows):
    low = lax.broadcasted_iota(jnp.int32, rows.shape, 1) < LANE_SPLIT
    zero = jnp.zeros_like(rows)
    return jnp.concatenate([jnp.where(low, rows, zero), jnp.where(low, zero, rows)], axis=0)


def one_row(stacked):
    half = stacked.shape[0] // 2
    low = lax.broadcasted_iota(jnp.int32, (half, stacked.shape[1]), 1) < LANE_SPLIT
    return jnp.where(low, stacked[:half], stacked[half:])


def document(refs, doc, block_total):
    source_ref, start_ref, count_ref = refs
    start = start_ref[doc]
    base = jnp.minimum(start, block_total - CAP)
    return source_ref[doc], base, start - base, count_ref[doc]


def forward_kernel(source_ref, start_ref, count_ref, q_ref, k_ref, v_ref, att_ref, w_ref, kept_ref, sems):
    att_ref[...] = jnp.zeros(att_ref.shape, att_ref.dtype)
    refs = (source_ref, start_ref, count_ref)
    lane = lax.broadcasted_iota(jnp.int32, (1, CAP * BLOCK), 1)
    copies = []
    for doc in range(DPS):
        source, base, skip, count = document(refs, doc, k_ref.shape[0] // BLOCK)
        tokens = pl.ds(pl.multiple_of(base * BLOCK, BLOCK), CAP * BLOCK)
        admitted = (lane >= skip * BLOCK) & (lane < (skip + count) * BLOCK)
        queries = two_heads(q_ref[source] * SCALE)
        scores = dot(queries, k_ref[tokens, :], ((1,), (1,)))
        scores = jnp.where(admitted, scores, MASKED)
        top = jnp.max(scores, axis=1, keepdims=True)
        terms = jnp.exp(scores - top)
        scale = 1.0 / jnp.sum(terms, axis=1, keepdims=True)
        weights = (terms * scale).astype(jnp.bfloat16)
        kept_ref[doc] = weights
        copies.append(pltpu.make_async_copy(kept_ref.at[doc], w_ref.at[doc], sems.at[doc]))
        copies[-1].start()
        mixed = dot(weights, v_ref[tokens, :], ((1,), (0,)))
        att_ref[source] = one_row(mixed).astype(jnp.bfloat16)
    for copy in copies:
        copy.wait()


def forward(source, start, count, got_q, keys, values):
    weights = (DPS, 2 * SLOT, CAP * BLOCK)
    return pl.pallas_call(
        forward_kernel,
        out_shape=(jax.ShapeDtypeStruct(got_q.shape, jnp.bfloat16), HBM(weights, jnp.bfloat16)),
        in_specs=smem_specs(3) + vmem_specs(3),
        out_specs=(*vmem_specs(1), pl.BlockSpec(memory_space=HBM)),
        scratch_shapes=[pltpu.VMEM(weights, jnp.bfloat16), pltpu.SemaphoreType.DMA((DPS,))],
        compiler_params=LIMIT,
        name="forward",
    )(source, start, count, got_q, keys, values)


def backward_kernel(
    source_ref, start_ref, count_ref, q_ref, g_ref, att_ref, w_ref, k_ref, v_ref, dq_ref, dk_ref, dv_ref
):
    dq_ref[...] = jnp.zeros(dq_ref.shape, dq_ref.dtype)
    refs = (source_ref, start_ref, count_ref)
    for doc in range(DPS):
        source, base, skip, _ = document(refs, doc, k_ref.shape[0] // BLOCK)
        tokens = pl.ds(pl.multiple_of(base * BLOCK, BLOCK), CAP * BLOCK)
        queries = two_heads(q_ref[source])
        grads = two_heads(g_ref[source])
        attended = att_ref[source].astype(jnp.float32)
        both = jnp.concatenate([attended, attended], axis=0)
        delta = jnp.sum(grads.astype(jnp.float32) * both, axis=1, keepdims=True)
        weights = w_ref[doc]
        dprobs = dot(grads, v_ref[tokens, :], ((1,), (1,)))
        dscores = (weights.astype(jnp.float32) * (dprobs - delta)).astype(jnp.bfloat16)
        dq = dot(dscores, k_ref[tokens, :], ((1,), (0,)))
        dq_ref[source] = (one_row(dq) * SCALE).astype(jnp.bfloat16)
        dk = (dot(dscores, queries, ((0,), (0,))) * SCALE).astype(jnp.bfloat16)
        dv = dot(weights, grads, ((0,), (0,))).astype(jnp.bfloat16)
        for part in range(CAP):
            rows = pl.ds(pl.multiple_of((base + part) * BLOCK, BLOCK), BLOCK)
            span = slice(part * BLOCK, (part + 1) * BLOCK)
            if part == CAP - 1:
                dk_ref[rows, :] = dk[span]
                dv_ref[rows, :] = dv[span]
            else:
                keep = skip > part
                dk_ref[rows, :] = jnp.where(keep, dk_ref[rows, :], dk[span])
                dv_ref[rows, :] = jnp.where(keep, dv_ref[rows, :], dv[span])


def backward(source, start, count, got_q, got_g, attended, weights, keys, values):
    return pl.pallas_call(
        backward_kernel,
        out_shape=(
            jax.ShapeDtypeStruct(got_q.shape, jnp.bfloat16),
            jax.ShapeDtypeStruct(keys.shape, jnp.bfloat16),
            jax.ShapeDtypeStruct(values.shape, jnp.bfloat16),
        ),
        in_specs=smem_specs(3) + vmem_specs(6),
        out_specs=tuple(vmem_specs(3)),
        compiler_params=LIMIT,
        name="backward",
    )(source, start, count, got_q, got_g, attended, weights, keys, values)


def mixed_kernel(start_ref, count_ref, head_ref, core_ref, packed_ref, proj_ref, *refs):
    first, second = refs[:SIDE], refs[SIDE : 2 * SIDE]
    outs = refs[2 * SIDE : 4 * SIDE]
    mine_ref, theirs_ref, sum_ref, sent_ref, weight_ref, other_ref, sems = refs[4 * SIDE :]
    unpack_rows(start_ref, count_ref, packed_ref, sum_ref)
    unit = sum_ref.shape[0] // (SIDE * SIDE)
    half = proj_ref.shape[1] // 2
    blocks = [
        [sum_ref[block_rows(head_ref, b, a, unit), :].astype(jnp.bfloat16) for b in range(SIDE)]
        for a in range(SIDE)
    ]
    rows = [jnp.concatenate(blocks[a], axis=0) for a in range(SIDE)]
    rows_two = [jnp.concatenate([blocks[a][b] for a in range(SIDE)], axis=0) for b in range(SIDE)]
    copies = []
    for h, part in enumerate((rows, rows_two)):
        cols = slice(h * half, (h + 1) * half)
        for p in (1, 3, 2, 0):
            place = h * SIDE + p
            sent_ref[place] = dot(part[p], proj_ref[:, cols], ((1,), (0,))).astype(jnp.bfloat16)
            copies.append(pltpu.make_async_copy(sent_ref.at[place], outs[place], sems.at[place]))
            copies[-1].start()
    sums = []
    for part, ins in ((rows, first), (rows_two, second)):
        term = None
        for p in range(SIDE):
            more = dot(part[p], ins[p][...], ((0,), (0,)))
            term = more if term is None else term + more
        sums.append(term)
    per_half = half // BLOCK
    for h in range(2):
        for c in range(per_half):
            chunk = h * per_half + c
            weight_ref[chunk % 2, chunk // 2] = sums[h][:, c * BLOCK : (c + 1) * BLOCK]
    core = core_ref[0]
    other_ref[...] = weight_ref[1 - core].astype(jnp.bfloat16)
    copies.append(pltpu.make_async_copy(other_ref, theirs_ref, sems.at[2 * SIDE]))
    copies[-1].start()
    copies.append(pltpu.make_async_copy(weight_ref.at[core], mine_ref, sems.at[2 * SIDE + 1]))
    copies[-1].start()
    for copy in copies:
        copy.wait()


def mixed_parts(start, count, head, core, packed, out_proj, first, second):
    inner, width = out_proj.shape
    row_count = SIDE * first[0].shape[0]
    part = HBM(first[0].shape, jnp.bfloat16)
    chunks = (width // BLOCK // 2, inner, BLOCK)
    outs = pl.pallas_call(
        mixed_kernel,
        out_shape=(part,) * (2 * SIDE) + (HBM(chunks, jnp.float32), HBM(chunks, jnp.bfloat16)),
        in_specs=smem_specs(4) + vmem_specs(2 + 2 * SIDE),
        out_specs=tuple([pl.BlockSpec(memory_space=HBM)] * (2 * SIDE + 2)),
        scratch_shapes=[
            pltpu.VMEM((row_count, inner), jnp.float32),
            pltpu.VMEM((2 * SIDE, *first[0].shape), jnp.bfloat16),
            pltpu.VMEM((2, *chunks), jnp.float32),
            pltpu.VMEM(chunks, jnp.bfloat16),
            pltpu.SemaphoreType.DMA((2 * SIDE + 2,)),
        ],
        compiler_params=LIMIT,
        name="mixed_parts",
    )(start, count, head, core, packed, out_proj, *first, *second)
    return outs[:SIDE], outs[SIDE : 2 * SIDE], outs[2 * SIDE], outs[2 * SIDE + 1]


def along_x(value, k):
    perm = [(x * SIDE + y, (x + k) % SIDE * SIDE + y) for x in range(SIDE) for y in range(SIDE)]
    return lax.ppermute(value, "head", perm)


def along_y(value, k):
    perm = [(x * SIDE + y, x * SIDE + (y + k) % SIDE) for x in range(SIDE) for y in range(SIDE)]
    return lax.ppermute(value, "head", perm)


def add_other(mine, theirs, distance):
    swap = [(s, s ^ distance) for s in range(N_SEQ)]
    other = lax.ppermute(theirs, "seq", swap)
    return mine + other.astype(jnp.float32)


def halve(low, high, side, distance):
    theirs = jnp.where(side == 0, high, low).astype(jnp.bfloat16)
    return add_other(jnp.where(side == 0, low, high), theirs, distance)


def shift(value, move, k):
    return move(value, k)


def gather(value, one, two):
    rows = jnp.concatenate([value] + [shift(value, one, k) for k in range(1, SIDE)], axis=0)
    return [rows] + [shift(rows, two, k) for k in range(1, SIDE)]


def total(parts):
    out = parts[0].astype(jnp.float32)
    for part in parts[1:]:
        out = out + part.astype(jnp.float32)
    return out.astype(jnp.bfloat16)


def scatter_sum(parts, one, two):
    terms = [parts[0]] + [shift(parts[k], one, SIDE - k) for k in range(1, SIDE)]
    rows = total(terms)
    unit = rows.shape[0] // SIDE
    terms = [rows[:unit]] + [
        shift(rows[k * unit : (k + 1) * unit], two, SIDE - k) for k in range(1, SIDE)
    ]
    return total(terms)


def to_all(value):
    return lax.all_to_all(value, "seq", split_axis=0, concat_axis=0, tiled=True)


def work(queries, enc_keys, enc_values, out_proj, out_grad, block_doc, query_doc):
    shard = lax.axis_index("seq")
    head = lax.axis_index("head").astype(jnp.int32)[None]
    row_count = queries.shape[0]
    half = out_grad.shape[1] // 2

    docs_here = lax.dynamic_slice_in_dim(query_doc, shard * row_count, row_count)
    slots = jnp.arange(N_SEQ, dtype=jnp.int32)[:, None]
    mine = docs_here[None, :] // DPS == slots
    rows = jnp.arange(row_count, dtype=jnp.int32)
    row_start = jnp.min(jnp.where(mine, rows[None, :], row_count - 1), axis=1)
    row_span = jnp.sum(mine.astype(jnp.int32), axis=1)
    got_q = to_all(pack_queries(row_start, row_span, queries))

    first = gather(out_grad[:, :half], along_x, along_y)
    second = gather(out_grad[:, half:], along_y, along_x)

    my_docs = shard * DPS + jnp.arange(DPS, dtype=jnp.int32)
    all_rows = jnp.arange(query_doc.shape[0], dtype=jnp.int32)
    source = jnp.max(jnp.where(query_doc[None, :] == my_docs[:, None], all_rows[None, :], 0), axis=1) // row_count
    local_blocks = enc_keys.shape[0] // BLOCK
    blocks_here = lax.dynamic_slice_in_dim(block_doc, shard * local_blocks, local_blocks)
    start = jnp.sum((blocks_here[None, :] < my_docs[:, None]).astype(jnp.int32), axis=1)
    count = jnp.sum((blocks_here[None, :] == my_docs[:, None]).astype(jnp.int32), axis=1)

    attended, weights = forward(source, start, count, got_q, enc_keys, enc_values)
    home = to_all(attended)
    got_g = to_all(attention_grads(row_start, row_span, head, out_proj, first, second))

    core = shard % 2
    m_first, m_second, mine, theirs = mixed_parts(row_start, row_span, head, core[None], home, out_proj, first, second)
    mixed = jnp.concatenate(
        [scatter_sum(m_first, along_y, along_x), scatter_sum(m_second, along_x, along_y)],
        axis=1,
    )

    chip = shard // 2
    grad_wo = add_other(mine, theirs, 1)
    for bit in range(3):
        halves = grad_wo.reshape(-1, 2, *grad_wo.shape[1:])
        grad_wo = halve(halves[:, 0], halves[:, 1], (chip >> bit) & 1, 2 << bit)
    grad_wo = grad_wo[0]

    grads_q, grad_k, grad_v = backward(
        source, start, count, got_q, got_g, attended, weights, enc_keys, enc_values
    )
    grad_q = unpack_grads(row_start, row_span, to_all(grads_q), row_count)
    return (mixed, grad_q, grad_k, grad_v, grad_wo)


def solution(mesh):
    placed = (
        P("seq", "head"),
        P("seq", "head"),
        P("seq", "head"),
        P("head", None),
        P(("seq", "head"), None),
        P(),
        P(),
    )
    return jax.shard_map(
        work,
        mesh=mesh,
        in_specs=placed,
        out_specs=(
            P(("seq", "head"), None),
            P("seq", "head"),
            P("seq", "head"),
            P("seq", "head"),
            P("head", "seq"),
        ),
        check_vma=False,
    )
```

```python
import jax
import jax.numpy as jnp
from jax import lax
from jax.experimental import pallas as pl
from jax.experimental.pallas import tpu as pltpu
from jax.sharding import PartitionSpec as P


BLOCK = 128
DPS = 8
SLOT = 144
TILE = 16
WINDOW = SLOT + TILE
CAP = 3
MASKED = -1e30
N_SEQ = 16
SIDE = 4
LANE_SPLIT = 64
SCALE = 0.125

VMEM = pltpu.MemorySpace.VMEM
SMEM = pltpu.MemorySpace.SMEM
HBM = pltpu.MemorySpace.HBM
LIMIT = pltpu.CompilerParams(vmem_limit_bytes=20 << 20)


def vmem_specs(count):
    return [pl.BlockSpec(memory_space=VMEM)] * count


def smem_specs(count):
    return [pl.BlockSpec(memory_space=SMEM)] * count


def dot(a, b, dims):
    return lax.dot_general(a, b, (dims, ((), ())), preferred_element_type=jnp.float32)


def select(equal):
    return jnp.where(equal, 1.0, 0.0).astype(jnp.bfloat16)


def window(start_ref, slot, row_count):
    start = start_ref[slot]
    base = pl.multiple_of(jnp.minimum(start // TILE * TILE, row_count - WINDOW), TILE)
    return pl.ds(base, WINDOW), start - base


def pack_rows(start_ref, count_ref, rows_ref, out_ref):
    lane = lax.broadcasted_iota(jnp.int32, (SLOT, WINDOW), 1)
    row = lax.broadcasted_iota(jnp.int32, (SLOT, WINDOW), 0)
    ahead = lane - row

    def step(slot, carry):
        span, skip = window(start_ref, slot, rows_ref.shape[0])
        chosen = select((ahead == skip) & (row < count_ref[slot]))
        out_ref[slot] = dot(chosen, rows_ref[span, :], ((1,), (0,))).astype(jnp.bfloat16)
        return carry

    lax.fori_loop(0, N_SEQ, step, 0, unroll=4)


def unpack_rows(start_ref, count_ref, packed_ref, sum_ref):
    lane = lax.broadcasted_iota(jnp.int32, (WINDOW, SLOT), 1)
    row = lax.broadcasted_iota(jnp.int32, (WINDOW, SLOT), 0)
    ahead = row - lane
    sum_ref[...] = jnp.zeros(sum_ref.shape, sum_ref.dtype)

    def step(slot, carry):
        span, skip = window(start_ref, slot, sum_ref.shape[0])
        chosen = select((ahead == skip) & (lane < count_ref[slot]))
        sum_ref[span, :] += dot(chosen, packed_ref[slot], ((1,), (0,)))
        return carry

    lax.fori_loop(0, N_SEQ, step, 0, unroll=4)


def block_rows(head_ref, behind_x, behind_y, unit):
    x, y = head_ref[0] // SIDE, head_ref[0] % SIDE
    block = (x + SIDE - behind_x) % SIDE * SIDE + (y + SIDE - behind_y) % SIDE
    return pl.ds(pl.multiple_of(block * unit, TILE), unit)


def pack_queries(start, count, queries):
    return pl.pallas_call(
        pack_rows,
        out_shape=jax.ShapeDtypeStruct((N_SEQ, SLOT, queries.shape[1]), jnp.bfloat16),
        in_specs=smem_specs(2) + vmem_specs(1),
        out_specs=pl.BlockSpec(memory_space=VMEM),
        compiler_params=LIMIT,
        name="pack_queries",
    )(start, count, queries)


def unpack_kernel(start_ref, count_ref, packed_ref, out_ref, sum_ref):
    unpack_rows(start_ref, count_ref, packed_ref, sum_ref)
    out_ref[...] = sum_ref[...].astype(jnp.bfloat16)


def unpack_grads(start, count, packed, row_count):
    shape = (row_count, packed.shape[2])
    return pl.pallas_call(
        unpack_kernel,
        out_shape=jax.ShapeDtypeStruct(shape, jnp.bfloat16),
        in_specs=smem_specs(2) + vmem_specs(1),
        out_specs=pl.BlockSpec(memory_space=VMEM),
        scratch_shapes=[pltpu.VMEM(shape, jnp.float32)],
        compiler_params=LIMIT,
        name="unpack_grads",
    )(start, count, packed)


def grad_kernel(start_ref, count_ref, head_ref, proj_ref, *refs):
    first, second, out_ref, rows_ref = refs[:SIDE], refs[SIDE : 2 * SIDE], refs[2 * SIDE], refs[2 * SIDE + 1]
    half = proj_ref.shape[1] // 2
    unit = rows_ref.shape[0] // (SIDE * SIDE)
    low = proj_ref[:, :half]
    high = proj_ref[:, half:]
    one = [dot(r[...], low, ((1,), (1,))) for r in first]
    two = [dot(r[...], high, ((1,), (1,))) for r in second]
    for a in range(SIDE):
        for b in range(SIDE):
            grads = one[a][b * unit : (b + 1) * unit] + two[b][a * unit : (a + 1) * unit]
            rows_ref[block_rows(head_ref, b, a, unit), :] = grads.astype(jnp.bfloat16)
    pack_rows(start_ref, count_ref, rows_ref, out_ref)


def attention_grads(start, count, head, out_proj, first, second):
    inner = out_proj.shape[0]
    row_count = SIDE * first[0].shape[0]
    return pl.pallas_call(
        grad_kernel,
        out_shape=jax.ShapeDtypeStruct((N_SEQ, SLOT, inner), jnp.bfloat16),
        in_specs=smem_specs(3) + vmem_specs(1 + 2 * SIDE),
        out_specs=pl.BlockSpec(memory_space=VMEM),
        scratch_shapes=[pltpu.VMEM((row_count, inner), jnp.bfloat16)],
        compiler_params=LIMIT,
        name="attention_grads",
    )(start, count, head, out_proj, *first, *second)


def two_heads(rows):
    low = lax.broadcasted_iota(jnp.int32, rows.shape, 1) < LANE_SPLIT
    zero = jnp.zeros_like(rows)
    return jnp.concatenate([jnp.where(low, rows, zero), jnp.where(low, zero, rows)], axis=0)


def one_row(stacked):
    half = stacked.shape[0] // 2
    low = lax.broadcasted_iota(jnp.int32, (half, stacked.shape[1]), 1) < LANE_SPLIT
    return jnp.where(low, stacked[:half], stacked[half:])


def document(refs, doc, block_total):
    source_ref, start_ref, count_ref = refs
    start = start_ref[doc]
    base = jnp.minimum(start, block_total - CAP)
    return source_ref[doc], base, start - base, count_ref[doc]


def forward_kernel(source_ref, start_ref, count_ref, q_ref, k_ref, v_ref, att_ref, w_ref, kept_ref, sems):
    att_ref[...] = jnp.zeros(att_ref.shape, att_ref.dtype)
    refs = (source_ref, start_ref, count_ref)
    lane = lax.broadcasted_iota(jnp.int32, (1, CAP * BLOCK), 1)
    copies = []
    for doc in range(DPS):
        source, base, skip, count = document(refs, doc, k_ref.shape[0] // BLOCK)
        tokens = pl.ds(pl.multiple_of(base * BLOCK, BLOCK), CAP * BLOCK)
        admitted = (lane >= skip * BLOCK) & (lane < (skip + count) * BLOCK)
        queries = two_heads(q_ref[source] * SCALE)
        scores = dot(queries, k_ref[tokens, :], ((1,), (1,)))
        scores = jnp.where(admitted, scores, MASKED)
        top = jnp.max(scores, axis=1, keepdims=True)
        terms = jnp.exp(scores - top)
        scale = 1.0 / jnp.sum(terms, axis=1, keepdims=True)
        weights = (terms * scale).astype(jnp.bfloat16)
        kept_ref[doc] = weights
        copies.append(pltpu.make_async_copy(kept_ref.at[doc], w_ref.at[doc], sems.at[doc]))
        copies[-1].start()
        mixed = dot(weights, v_ref[tokens, :], ((1,), (0,)))
        att_ref[source] = one_row(mixed).astype(jnp.bfloat16)
    for copy in copies:
        copy.wait()


def forward(source, start, count, got_q, keys, values):
    weights = (DPS, 2 * SLOT, CAP * BLOCK)
    return pl.pallas_call(
        forward_kernel,
        out_shape=(jax.ShapeDtypeStruct(got_q.shape, jnp.bfloat16), HBM(weights, jnp.bfloat16)),
        in_specs=smem_specs(3) + vmem_specs(3),
        out_specs=(*vmem_specs(1), pl.BlockSpec(memory_space=HBM)),
        scratch_shapes=[pltpu.VMEM(weights, jnp.bfloat16), pltpu.SemaphoreType.DMA((DPS,))],
        compiler_params=LIMIT,
        name="forward",
    )(source, start, count, got_q, keys, values)


def backward_kernel(
    source_ref, start_ref, count_ref, q_ref, g_ref, att_ref, w_ref, k_ref, v_ref, dq_ref, dk_ref, dv_ref
):
    dq_ref[...] = jnp.zeros(dq_ref.shape, dq_ref.dtype)
    refs = (source_ref, start_ref, count_ref)
    for doc in range(DPS):
        source, base, skip, _ = document(refs, doc, k_ref.shape[0] // BLOCK)
        tokens = pl.ds(pl.multiple_of(base * BLOCK, BLOCK), CAP * BLOCK)
        queries = two_heads(q_ref[source])
        grads = two_heads(g_ref[source])
        attended = att_ref[source].astype(jnp.float32)
        both = jnp.concatenate([attended, attended], axis=0)
        delta = jnp.sum(grads.astype(jnp.float32) * both, axis=1, keepdims=True)
        weights = w_ref[doc]
        dprobs = dot(grads, v_ref[tokens, :], ((1,), (1,)))
        dscores = (weights.astype(jnp.float32) * (dprobs - delta)).astype(jnp.bfloat16)
        dq = dot(dscores, k_ref[tokens, :], ((1,), (0,)))
        dq_ref[source] = (one_row(dq) * SCALE).astype(jnp.bfloat16)
        dk = (dot(dscores, queries, ((0,), (0,))) * SCALE).astype(jnp.bfloat16)
        dv = dot(weights, grads, ((0,), (0,))).astype(jnp.bfloat16)
        for part in range(CAP):
            rows = pl.ds(pl.multiple_of((base + part) * BLOCK, BLOCK), BLOCK)
            span = slice(part * BLOCK, (part + 1) * BLOCK)
            if part == CAP - 1:
                dk_ref[rows, :] = dk[span]
                dv_ref[rows, :] = dv[span]
            else:
                keep = skip > part
                dk_ref[rows, :] = jnp.where(keep, dk_ref[rows, :], dk[span])
                dv_ref[rows, :] = jnp.where(keep, dv_ref[rows, :], dv[span])


def backward(source, start, count, got_q, got_g, attended, weights, keys, values):
    return pl.pallas_call(
        backward_kernel,
        out_shape=(
            jax.ShapeDtypeStruct(got_q.shape, jnp.bfloat16),
            jax.ShapeDtypeStruct(keys.shape, jnp.bfloat16),
            jax.ShapeDtypeStruct(values.shape, jnp.bfloat16),
        ),
        in_specs=smem_specs(3) + vmem_specs(6),
        out_specs=tuple(vmem_specs(3)),
        compiler_params=LIMIT,
        name="backward",
    )(source, start, count, got_q, got_g, attended, weights, keys, values)


def mixed_kernel(start_ref, count_ref, head_ref, core_ref, packed_ref, proj_ref, *refs):
    first, second = refs[:SIDE], refs[SIDE : 2 * SIDE]
    outs = refs[2 * SIDE : 4 * SIDE]
    mine_ref, theirs_ref, sum_ref, sent_ref, weight_ref, other_ref, sems = refs[4 * SIDE :]
    unpack_rows(start_ref, count_ref, packed_ref, sum_ref)
    unit = sum_ref.shape[0] // (SIDE * SIDE)
    half = proj_ref.shape[1] // 2
    blocks = [
        [sum_ref[block_rows(head_ref, b, a, unit), :].astype(jnp.bfloat16) for b in range(SIDE)]
        for a in range(SIDE)
    ]
    rows = [jnp.concatenate(blocks[a], axis=0) for a in range(SIDE)]
    rows_two = [jnp.concatenate([blocks[a][b] for a in range(SIDE)], axis=0) for b in range(SIDE)]
    copies = []
    for h, part in enumerate((rows, rows_two)):
        cols = slice(h * half, (h + 1) * half)
        for p in (1, 3, 2, 0):
            place = h * SIDE + p
            sent_ref[place] = dot(part[p], proj_ref[:, cols], ((1,), (0,))).astype(jnp.bfloat16)
            copies.append(pltpu.make_async_copy(sent_ref.at[place], outs[place], sems.at[place]))
            copies[-1].start()
    sums = []
    for part, ins in ((rows, first), (rows_two, second)):
        term = None
        for p in range(SIDE):
            more = dot(part[p], ins[p][...], ((0,), (0,)))
            term = more if term is None else term + more
        sums.append(term)
    per_half = half // BLOCK
    for h in range(2):
        for c in range(per_half):
            chunk = h * per_half + c
            weight_ref[chunk % 2, chunk // 2] = sums[h][:, c * BLOCK : (c + 1) * BLOCK]
    core = core_ref[0]
    other_ref[...] = weight_ref[1 - core].astype(jnp.bfloat16)
    copies.append(pltpu.make_async_copy(other_ref, theirs_ref, sems.at[2 * SIDE]))
    copies[-1].start()
    copies.append(pltpu.make_async_copy(weight_ref.at[core], mine_ref, sems.at[2 * SIDE + 1]))
    copies[-1].start()
    for copy in copies:
        copy.wait()


def mixed_parts(start, count, head, core, packed, out_proj, first, second):
    inner, width = out_proj.shape
    row_count = SIDE * first[0].shape[0]
    part = HBM(first[0].shape, jnp.bfloat16)
    chunks = (width // BLOCK // 2, inner, BLOCK)
    outs = pl.pallas_call(
        mixed_kernel,
        out_shape=(part,) * (2 * SIDE) + (HBM(chunks, jnp.float32), HBM(chunks, jnp.bfloat16)),
        in_specs=smem_specs(4) + vmem_specs(2 + 2 * SIDE),
        out_specs=tuple([pl.BlockSpec(memory_space=HBM)] * (2 * SIDE + 2)),
        scratch_shapes=[
            pltpu.VMEM((row_count, inner), jnp.float32),
            pltpu.VMEM((2 * SIDE, *first[0].shape), jnp.bfloat16),
            pltpu.VMEM((2, *chunks), jnp.float32),
            pltpu.VMEM(chunks, jnp.bfloat16),
            pltpu.SemaphoreType.DMA((2 * SIDE + 2,)),
        ],
        compiler_params=LIMIT,
        name="mixed_parts",
    )(start, count, head, core, packed, out_proj, *first, *second)
    return outs[:SIDE], outs[SIDE : 2 * SIDE], outs[2 * SIDE], outs[2 * SIDE + 1]


def along_x(value, k):
    perm = [(x * SIDE + y, (x + k) % SIDE * SIDE + y) for x in range(SIDE) for y in range(SIDE)]
    return lax.ppermute(value, "head", perm)


def along_y(value, k):
    perm = [(x * SIDE + y, x * SIDE + (y + k) % SIDE) for x in range(SIDE) for y in range(SIDE)]
    return lax.ppermute(value, "head", perm)


def add_other(mine, theirs, distance):
    swap = [(s, s ^ distance) for s in range(N_SEQ)]
    other = lax.ppermute(theirs, "seq", swap)
    return mine + other.astype(jnp.float32)


def halve(low, high, side, distance):
    theirs = jnp.where(side == 0, high, low).astype(jnp.bfloat16)
    return add_other(jnp.where(side == 0, low, high), theirs, distance)


def shift(value, move, k):
    return move(value, k)


def gather(value, one, two):
    rows = jnp.concatenate([value] + [shift(value, one, k) for k in range(1, SIDE)], axis=0)
    return [rows] + [shift(rows, two, k) for k in range(1, SIDE)]


def total(parts):
    out = parts[0].astype(jnp.float32)
    for part in parts[1:]:
        out = out + part.astype(jnp.float32)
    return out.astype(jnp.bfloat16)


def scatter_sum(parts, one, two):
    terms = [parts[0]] + [shift(parts[k], one, SIDE - k) for k in range(1, SIDE)]
    rows = total(terms)
    unit = rows.shape[0] // SIDE
    terms = [rows[:unit]] + [
        shift(rows[k * unit : (k + 1) * unit], two, SIDE - k) for k in range(1, SIDE)
    ]
    return terms


def to_all(value):
    return lax.all_to_all(value, "seq", split_axis=0, concat_axis=0, tiled=True)


def work(queries, enc_keys, enc_values, out_proj, out_grad, block_doc, query_doc):
    shard = lax.axis_index("seq")
    head = lax.axis_index("head").astype(jnp.int32)[None]
    row_count = queries.shape[0]
    half = out_grad.shape[1] // 2

    docs_here = lax.dynamic_slice_in_dim(query_doc, shard * row_count, row_count)
    slots = jnp.arange(N_SEQ, dtype=jnp.int32)[:, None]
    mine = docs_here[None, :] // DPS == slots
    rows = jnp.arange(row_count, dtype=jnp.int32)
    row_start = jnp.min(jnp.where(mine, rows[None, :], row_count - 1), axis=1)
    row_span = jnp.sum(mine.astype(jnp.int32), axis=1)
    got_q = to_all(pack_queries(row_start, row_span, queries))

    first = gather(out_grad[:, :half], along_x, along_y)
    second = gather(out_grad[:, half:], along_y, along_x)

    my_docs = shard * DPS + jnp.arange(DPS, dtype=jnp.int32)
    all_rows = jnp.arange(query_doc.shape[0], dtype=jnp.int32)
    source = jnp.max(jnp.where(query_doc[None, :] == my_docs[:, None], all_rows[None, :], 0), axis=1) // row_count
    local_blocks = enc_keys.shape[0] // BLOCK
    blocks_here = lax.dynamic_slice_in_dim(block_doc, shard * local_blocks, local_blocks)
    start = jnp.sum((blocks_here[None, :] < my_docs[:, None]).astype(jnp.int32), axis=1)
    count = jnp.sum((blocks_here[None, :] == my_docs[:, None]).astype(jnp.int32), axis=1)

    attended, weights = forward(source, start, count, got_q, enc_keys, enc_values)
    home = to_all(attended)
    got_g = to_all(attention_grads(row_start, row_span, head, out_proj, first, second))

    core = shard % 2
    m_first, m_second, mine, theirs = mixed_parts(row_start, row_span, head, core[None], home, out_proj, first, second)
    m_first = scatter_sum(m_first, along_y, along_x)
    m_second = scatter_sum(m_second, along_x, along_y)
    mixed = total([jnp.concatenate(pair, axis=1) for pair in zip(m_first, m_second)])

    chip = shard // 2
    grad_wo = add_other(mine, theirs, 1)
    for bit in range(3):
        halves = grad_wo.reshape(-1, 2, *grad_wo.shape[1:])
        grad_wo = halve(halves[:, 0], halves[:, 1], (chip >> bit) & 1, 2 << bit)
    grad_wo = grad_wo[0]

    grads_q, grad_k, grad_v = backward(
        source, start, count, got_q, got_g, attended, weights, enc_keys, enc_values
    )
    grad_q = unpack_grads(row_start, row_span, to_all(grads_q), row_count)
    return (mixed, grad_q, grad_k, grad_v, grad_wo)


def solution(mesh):
    placed = (
        P("seq", "head"),
        P("seq", "head"),
        P("seq", "head"),
        P("head", None),
        P(("seq", "head"), None),
        P(),
        P(),
    )
    return jax.shard_map(
        work,
        mesh=mesh,
        in_specs=placed,
        out_specs=(
            P(("seq", "head"), None),
            P("seq", "head"),
            P("seq", "head"),
            P("seq", "head"),
            P("head", "seq"),
        ),
        check_vma=False,
    )
```
